512 devices in a mesh: dp: 8 (over z), section: 4 (over x), tm: 16 (over y, core).
Axes of the slice: x: 4, y: 8, z: 8, core: 2. Of those that a mesh axis runs over, the one named last changes fastest.
Arguments:
- frames: bfloat16 [16, 2048, 1280], P('dp', 'tm'), may hold values from -6 to 6
- block_mask: int32 [16, 32, 2], P('dp', 'tm'), may hold values 0 or 1
- span_segment: int32 [16, 32], P('dp'), may hold values from 0 to 15, as said below
- dec_states: bfloat16 [8192, 1280], P(('dp', 'tm')), may hold values from -6 to 6
- enc_qkv: bfloat16 [4, 1280, 1920], P('section', ('dp', 'tm')), may hold values from -0.15625 to 0.15625
- enc_out: bfloat16 [4, 640, 1280], P('section', None, ('dp', 'tm')), may hold values from -0.75 to 0.75
- cross_query: bfloat16 [1280, 768], P(('dp', 'tm'), 'section'), may hold values from -0.15625 to 0.15625
- cross_key: bfloat16 [1280, 768], P(('dp', 'tm'), 'section'), may hold values from -0.15625 to 0.15625
- cross_value: bfloat16 [1280, 768], P(('dp', 'tm'), 'section'), may hold values from -0.75 to 0.75
- cotangent: bfloat16 [8192, 1280], P(('dp', 'tm')), may hold values from -1 to 1
Outputs:
- context: bfloat16 [8192, 768], P(('dp', 'tm'), 'section')
- out_grad: float32 [768, 1280], P('section', ('dp', 'tm'))
The draws below stay inside these ranges and needn't reach their ends.
Inputs may be any that keep to these rules, and one draw needn't show every extreme that they name: `span_segment`: the first of every 2 blocks, block d * 2, serves segment (d + 8) mod 16; every other block serves a segment drawn evenly.
All inputs are finite; a program needn't handle non-finite values. No bound on the sum of `block_mask` on one device may be relied on, other than what follows from the above.
Results may differ from the reference program's by a relative error of at most 0.011.
Values may be sent and summed in bfloat16 or wider, within the bound.
No kernel may reach another device: no remote copies, remote signals or barrier semaphores. Data moves between devices by JAX's collectives and lax.ppermute only.
A program may use at most 64 MiB of HBM per device.

```python
import jax
import jax.numpy as jnp
from jax import lax

D = 1280
HD = 64
ENC_HEADS = 10
BLK = 64
MB = 2
TF = 128
DTOK = 32
SEQS = 16
FRAMES = 2048
NBLK = 32
CROSS_HEADS = 12
TOKALL = 8192
N_DP = 8
N_SECTION = 4
N_TM = 16


def draw_span_segment(key, part):
    drawn = jax.random.randint(key, (SEQS, NBLK), 0, N_TM, dtype=jnp.int32)
    block_index = jnp.arange(NBLK, dtype=jnp.int32)
    per_shard = TF // BLK
    shard_of = block_index // per_shard
    leading = block_index % per_shard == 0
    opposite = (shard_of + N_TM // 2) % N_TM
    return jnp.where(leading[None, :], opposite[None, :], drawn).astype(jnp.int32)


def set_ends(values, stream_key, least, top_value):
    longest = values.shape.index(max(values.shape))
    spots = []
    for shift in (0, 1):
        where = [jax.random.randint(jax.random.fold_in(stream_key, axis), (), 0, length) for axis, length in enumerate(values.shape)]
        where[longest] = (where[longest] + shift) % values.shape[longest]
        spots.append(tuple(where))
    return values.at[spots[0]].set(least).at[spots[1]].set(top_value)


def strengthened(entries, own_key, source, target, shards_of, factor):
    def block_of(dim):
        return (jnp.arange(entries.shape[dim]) // (entries.shape[dim] // shards_of)).reshape((-1,) + (1,) * (entries.ndim - 1 - dim))

    one_side = jax.random.permutation(own_key, shards_of)[block_of(target)]
    other_side = (block_of(target) + shards_of // 2) % shards_of
    return jnp.where((block_of(source) == one_side) | (block_of(source) == other_side), factor * entries, entries)


def block_levels(stream_key, shape, shards, smallest, top_value):
    gain, own = 1.0, jax.random.fold_in(stream_key, 6)
    for position, blocks in shards:
        heights = jnp.exp(jax.random.uniform(jax.random.fold_in(own, position), (blocks,), jnp.float32, smallest / len(shards), top_value / len(shards)))
        gain = gain * jnp.repeat(heights, shape[position] // blocks).reshape([-1 if axis == position else 1 for axis in range(len(shape))])
    return gain


def bell_draw(stream_key, shape, width, limit, shards=(), held_as=jnp.bfloat16):
    loudness = block_levels(stream_key, shape, shards, -0.22, 0.18) if shards else 1.0
    values = jax.random.normal(stream_key, shape, jnp.float32) * width * loudness
    return jnp.minimum(jnp.maximum(values, -limit), limit).astype(held_as)


def heavy_noise(own_key, dims, scale, limit, cuts, heavy, kind=jnp.bfloat16):
    result = scale * jax.random.normal(own_key, dims, jnp.float32)
    if cuts:
        result = result * block_levels(own_key, dims, cuts, -0.22, 0.18)
    return jnp.clip(strengthened(result, jax.random.fold_in(own_key, 3), *heavy), -limit, limit).astype(kind)


def setup_inputs(seed: int = 0) -> dict:
    splits = jax.random.split(jax.random.key(seed), 11)
    return {
        "frames": bell_draw(splits[0], (SEQS, FRAMES, D), 1.0, 6.0, ((0, 8), (1, 16))),
        "block_mask": set_ends((jax.random.randint(splits[1], (SEQS, NBLK, 2), 0, 2) < 1).astype(jnp.int32), jax.random.fold_in(splits[1], 1), 0, 1),
        "span_segment": draw_span_segment(jax.random.fold_in(splits[10], 71), 0),
        "dec_states": bell_draw(splits[3], (TOKALL, D), 1.0, 6.0, ((0, 128),)),
        "enc_qkv": bell_draw(splits[4], (N_SECTION, D, 3 * ENC_HEADS * HD), D ** -0.5, 0.15625, ((0, 4), (1, 128))),
        "enc_out": bell_draw(splits[5], (N_SECTION, ENC_HEADS * HD, D), HD ** -0.5, 0.75, ((0, 4), (2, 128))),
        "cross_query": bell_draw(splits[6], (D, CROSS_HEADS * HD), D ** -0.5, 0.15625, ((0, 128), (1, 4))),
        "cross_key": bell_draw(splits[7], (D, CROSS_HEADS * HD), D ** -0.5, 0.15625, ((0, 128), (1, 4))),
        "cross_value": bell_draw(splits[8], (D, CROSS_HEADS * HD), HD ** -0.5, 0.75, ((0, 128), (1, 4))),
        "cotangent": heavy_noise(splits[9], (TOKALL, D), (4.0 * TOKALL ** -0.5), 1.0, ((0, 128),), (0, 1, 128, 5.5)),
    }


epsilon = 1e-05

def norm_rows(inputs):
    values32 = inputs.astype(jnp.float32)
    center = values32 - lax.optimization_barrier(jnp.mean(values32, axis=-1, keepdims=True))
    spread = lax.optimization_barrier(jnp.mean(center * center, axis=-1, keepdims=True))
    return (center * lax.rsqrt(spread + epsilon)).astype(jnp.bfloat16)

def allowed_keys(mask_rows, first_block, total_blocks):
    block_count = mask_rows.shape[0]
    block_index = first_block + jnp.arange(block_count, dtype=jnp.int32)
    left_open = (mask_rows[:, 0] == 1) & (block_index > 0)
    right_open = (mask_rows[:, 1] == 1) & (block_index < total_blocks - 1)
    middle = jnp.ones((block_count, BLK), dtype=jnp.bool_)
    return jnp.concatenate([jnp.broadcast_to(left_open[:, None], (block_count, BLK)), middle, jnp.broadcast_to(right_open[:, None], (block_count, BLK))], axis=1)

def window_attention(queries, key_rows, value_rows, allowed):
    frame_count = queries.shape[0]
    block_count = frame_count // BLK
    head_count = queries.shape[1] // HD

    def windows(padded):
        return jnp.concatenate([padded[offset * BLK:offset * BLK + frame_count].reshape(block_count, BLK, head_count, HD) for offset in range(3)], axis=1)
    query_blocks = queries.reshape(block_count, BLK, head_count, HD).astype(jnp.float32)
    scores = jnp.einsum('bqhd,bkhd->bhqk', query_blocks, windows(key_rows).astype(jnp.float32)) * HD ** (-0.5)
    weights = jnp.where(allowed[:, None, None, :], jnp.exp(scores), 0.0)
    totals = lax.optimization_barrier(jnp.sum(weights, axis=-1))
    summed = jnp.einsum('bhqk,bkhd->bqhd', weights.astype(jnp.bfloat16).astype(jnp.float32), windows(value_rows).astype(jnp.float32))
    context = summed / jnp.transpose(totals, (0, 2, 1))[..., None]
    return context.reshape(frame_count, head_count * HD).astype(jnp.bfloat16)

def encoder_layer(hidden, mask_rows, proj_qkv, proj_out):
    enc_width = proj_out.shape[0]
    normed = norm_rows(hidden)
    packed = jnp.dot(normed, proj_qkv, preferred_element_type=jnp.float32).astype(jnp.bfloat16)
    border = jnp.zeros((BLK, 2 * enc_width), jnp.bfloat16)
    key_value = jnp.concatenate([border, packed[:, enc_width:], border], axis=0)
    allowed = allowed_keys(mask_rows, 0, mask_rows.shape[0])
    context = window_attention(packed[:, :enc_width], key_value[:, :enc_width], key_value[:, enc_width:], allowed)
    update = jnp.dot(context, proj_out, preferred_element_type=jnp.float32)
    return (hidden.astype(jnp.float32) + update).astype(jnp.bfloat16)

def reference(frames, block_mask, span_segment, dec_states, enc_qkv, enc_out, cross_query, cross_key, cross_value, cotangent):

    def encode(operands):
        hidden, mask_rows = operands
        for section_layer in range(N_SECTION):
            hidden = encoder_layer(hidden, mask_rows, enc_qkv[section_layer], enc_out[section_layer])
        return hidden
    memory = lax.map(encode, (frames, block_mask))
    decoder = dec_states.reshape(N_DP, N_TM, MB, DTOK, D).transpose(0, 2, 1, 3, 4).reshape(SEQS, N_TM * DTOK, D)
    query_segment = jnp.arange(N_TM * DTOK, dtype=jnp.int32) // DTOK
    head_count = CROSS_HEADS

    def cross(operands):
        memory_rows, decoder_rows, segment_rows = operands
        mem_norm = norm_rows(memory_rows)
        key_rows = jnp.dot(mem_norm, cross_key, preferred_element_type=jnp.float32).astype(jnp.bfloat16)
        value_rows = jnp.dot(mem_norm, cross_value, preferred_element_type=jnp.float32).astype(jnp.bfloat16)
        query_rows = jnp.dot(norm_rows(decoder_rows), cross_query, preferred_element_type=jnp.float32).astype(jnp.bfloat16)
        frame_segment = jnp.repeat(segment_rows, BLK)
        allowed = query_segment[:, None] == frame_segment[None, :]

        def one_head(head_operands):
            head_query, head_key, head_value = head_operands
            scores = jnp.dot(head_query, head_key.T, preferred_element_type=jnp.float32) * HD ** (-0.5)
            weights = jnp.where(allowed, jnp.exp(scores), 0.0)
            totals = lax.optimization_barrier(jnp.sum(weights, axis=-1))
            summed = jnp.dot(weights.astype(jnp.bfloat16), head_value, preferred_element_type=jnp.float32)
            return summed / totals[:, None]
        split_query = query_rows.reshape(-1, head_count, HD).transpose(1, 0, 2)
        split_key = key_rows.reshape(-1, head_count, HD).transpose(1, 0, 2)
        split_value = value_rows.reshape(-1, head_count, HD).transpose(1, 0, 2)
        context = lax.map(one_head, (split_query, split_key, split_value))
        return context.transpose(1, 0, 2).reshape(-1, head_count * HD).astype(jnp.bfloat16)
    context_all = lax.map(cross, (memory, decoder, span_segment))
    context = context_all.reshape(N_DP, MB, N_TM, DTOK, CROSS_HEADS * HD).transpose(0, 2, 1, 3, 4)
    context = context.reshape(TOKALL, CROSS_HEADS * HD)
    out_grad = jnp.dot(context.T, cotangent, preferred_element_type=jnp.float32)
    return (context, out_grad)
```

```python
import functools

import jax
import jax.numpy as jnp
from jax import lax
from jax.experimental import pallas as pl
from jax.experimental.pallas import tpu as pltpu
from jax.sharding import PartitionSpec as P

HD = 64
BLK = 64
MB = 2
EPS = 1e-05
F32 = jnp.float32
BF16 = jnp.bfloat16
VMEM = pl.BlockSpec(memory_space=pltpu.VMEM)
SMEM = pl.BlockSpec(memory_space=pltpu.SMEM)
PARAMS = pltpu.CompilerParams(vmem_limit_bytes=16 * 1024 * 1024)
JOIN_PARAMS = pltpu.CompilerParams()
JOINED = VMEM


def normed_rows(values):
    wide = values.astype(F32)
    center = wide - jnp.mean(wide, axis=-1, keepdims=True)
    spread = jnp.mean(center * center, axis=-1, keepdims=True)
    return (center * lax.rsqrt(spread + EPS)).astype(BF16)


def matmul(a, b):
    return jnp.dot(a, b, preferred_element_type=F32)


def matmul_nt(a, b):
    return lax.dot_general(a, b, (((1,), (1,)), ((), ())), preferred_element_type=F32)


def join_kernel(*refs):
    pieces, outs, sems = refs[:-4], refs[-4:-1], refs[-1]
    copies = []
    start = 0
    for index, out_ref in enumerate(outs):
        cols = slice(start, start + out_ref.shape[1])
        start += out_ref.shape[1]
        for slot, piece in enumerate(pieces):
            height = piece.shape[0]
            copies.append(
                pltpu.make_async_copy(
                    piece.at[:, cols],
                    out_ref.at[pl.ds(slot * height, height), :],
                    sems.at[index, slot],
                )
            )
    for copy in copies:
        copy.start()
    for copy in copies:
        copy.wait()


def kv_kernel(x_ref, w_ref, n_ref, first_ref, last_ref):
    n = normed_rows(x_ref[...])
    n_ref[...] = n
    kv = matmul(n, w_ref[...]).astype(BF16)
    first_ref[...] = kv[:BLK]
    last_ref[...] = kv[BLK:]


def allowed_of(moment, halo, place_ref, mask_ref):
    base = 4 * jnp.clip(moment - place_ref[0], 0, MB - 1)
    shard = place_ref[2]
    row = lax.broadcasted_iota(jnp.int32, (4 * BLK, 2 * BLK), 0)
    col = lax.broadcasted_iota(jnp.int32, (4 * BLK, 2 * BLK), 1)
    same = ((row // BLK) % 2 == 0) == (col < BLK)
    low_row = (row // BLK) % 2 == 0
    if halo:
        before = jnp.where(shard > 0, mask_ref[base], 0)
        after = jnp.where(shard < place_ref[5], mask_ref[base + 3], 0)
        open_side = jnp.where(low_row, before, after) == 1
        return same & open_side
    open_side = jnp.where(low_row, mask_ref[base + 1], mask_ref[base + 2]) == 1
    return same | open_side


def pair_attention(q, k, v, allowed):
    rows = q.shape[0]
    low = lax.broadcasted_iota(jnp.int32, q.shape, 1) < HD
    zero = jnp.zeros_like(q)
    both = jnp.concatenate([jnp.where(low, q, zero), jnp.where(low, zero, q)], axis=0)
    scores = matmul_nt(both, k) * HD ** (-0.5)
    weights = jnp.where(allowed, jnp.exp(scores), 0.0)
    totals = jnp.sum(weights, axis=-1, keepdims=True)
    summed = matmul(weights.astype(BF16), v)
    return (
        jnp.where(low, summed[:rows], summed[rows:]),
        jnp.where(low, totals[:rows], totals[rows:]),
    )


def own_kernel(
    moment, place_ref, mask_ref, n_ref, first_ref, last_ref, w_ref, q_ref, num_ref, den_ref
):
    width = q_ref.shape[1]
    allowed = allowed_of(moment, False, place_ref, mask_ref)
    q = matmul(n_ref[...], w_ref[...]).astype(BF16)
    q_ref[...] = q
    for lane in range(0, width, 2 * HD):
        cols = slice(lane, lane + 2 * HD)
        vcols = slice(width + lane, width + lane + 2 * HD)
        k = jnp.concatenate([first_ref[:, cols], last_ref[:, cols]], axis=0)
        v = jnp.concatenate([first_ref[:, vcols], last_ref[:, vcols]], axis=0)
        num_ref[:, cols], den_ref[:, cols] = pair_attention(q[:, cols], k, v, allowed)


def out_kernel(
    moment, place_ref, mask_ref, q_ref, num_ref, den_ref, left_ref, right_ref, x_ref, w_ref,
    o_ref, ctx_ref
):
    width = q_ref.shape[1]
    allowed = allowed_of(moment, True, place_ref, mask_ref)
    for lane in range(0, width, 2 * HD):
        cols = slice(lane, lane + 2 * HD)
        vcols = slice(width + lane, width + lane + 2 * HD)
        k = jnp.concatenate([left_ref[:, cols], right_ref[:, cols]], axis=0)
        v = jnp.concatenate([left_ref[:, vcols], right_ref[:, vcols]], axis=0)
        num, den = pair_attention(q_ref[:, cols], k, v, allowed)
        ctx_ref[:, cols] = ((num + num_ref[:, cols]) / (den + den_ref[:, cols])).astype(BF16)
    update = matmul_nt(ctx_ref[...], w_ref[...])
    o_ref[...] = (x_ref[...].astype(F32) + update).astype(BF16)


def order_kernel(order_ref, frames_ref, *out_refs):
    seqs, rows, model = frames_ref.shape
    frames = frames_ref[...].reshape(seqs * rows, model)
    for lane in range(0, model, 256):
        source = lax.broadcasted_iota(jnp.int32, (model, 256), 0)
        hit = source == order_ref[:, lane : lane + 256]
        pick = jnp.where(hit, 1.0, 0.0).astype(BF16)
        moved = matmul(frames, pick).astype(BF16)
        for seq, out_ref in enumerate(out_refs):
            out_ref[:, lane : lane + 256] = moved[seq * rows : (seq + 1) * rows]


def reorder_kernel(order_ref, w_ref, out_ref):
    model = w_ref.shape[0]
    for row in range(0, model, 256):
        source = lax.broadcasted_iota(jnp.int32, (256, model), 1)
        hit = source == order_ref[row : row + 256, :]
        pick = jnp.where(hit, 1.0, 0.0).astype(BF16)
        out_ref[row : row + 256, :] = matmul(pick, w_ref[...]).astype(BF16)


def query_kernel(seg_ref, dec_ref, w_ref, q_ref):
    q_ref[...] = matmul(normed_rows(dec_ref[...]), w_ref[...]).astype(BF16)


def cross_kernel(place_ref, q_ref, w_ref, *refs):
    parts, out_ref = refs[:-1], refs[-1]
    owner = place_ref[0] == place_ref[1]
    rows = []
    for start in (0, 4):
        own, a, b, c = (ref[...] for ref in parts[start : start + 4])
        rows.append(jnp.where(owner, own, a + b + c))
    n = normed_rows(jnp.concatenate(rows, axis=0))
    width = q_ref.shape[1]
    both = matmul(n, w_ref[...]).astype(BF16)
    keys, values = both[:, :width], both[:, width:]
    tokens = q_ref.shape[0] // 4
    heads = 3
    lane = lax.broadcasted_iota(jnp.int32, (tokens, width), 1)
    near = lax.broadcasted_iota(jnp.int32, (tokens, 2 * HD), 1)
    sums = jnp.zeros((tokens, 2 * HD), F32)
    thirds = []
    for piece in range(4):
        q = q_ref[piece * tokens : (piece + 1) * tokens, :]
        spots = slice(piece * BLK, (piece + 1) * BLK)
        stacked = jnp.concatenate(
            [jnp.where(lane // HD == head, q, jnp.zeros_like(q)) for head in range(heads)], axis=0
        )
        weights = jnp.exp(matmul_nt(stacked, keys[spots]) * HD ** (-0.5))
        totals = jnp.sum(weights, axis=-1, keepdims=True)
        summed = matmul(weights.astype(BF16), values[spots])
        high = totals.astype(BF16).astype(F32)
        rest = totals - high
        for head in range(heads):
            mine = slice(head * tokens, (head + 1) * tokens)
            sums = jnp.where(near == 32 * piece + head, high[mine], sums)
            sums = jnp.where(near == 32 * piece + heads + head, rest[mine], sums)
        pair = jnp.where(near < HD, summed[:tokens, : 2 * HD], summed[tokens : 2 * tokens, : 2 * HD])
        out_ref[piece * tokens : (piece + 1) * tokens, :] = pair.astype(BF16)
        thirds.append(summed[2 * tokens :, 2 * HD :])
    at = 4 * tokens
    for block in range(2):
        shifted = pltpu.roll(thirds[2 + block], HD, 1)
        out_ref[at + block * tokens : at + (block + 1) * tokens, :] = jnp.where(
            near < HD, thirds[block], shifted
        ).astype(BF16)
    out_ref[at + 2 * tokens :, :] = sums.astype(BF16)


def combine_kernel(
    place_ref, span_ref, parts_ref, cot_ref, ctx_ref, grad_ref, pair_ref, third_ref, sum_ref, all_ref
):
    shards = parts_ref.shape[0]
    tokens = pair_ref.shape[1]
    heads = 3
    for ref in (pair_ref, third_ref, sum_ref):
        ref[...] = jnp.zeros_like(ref)
    lane = lax.broadcasted_iota(jnp.int32, (tokens, 2 * HD), 1)
    for shard in range(shards):
        sums = parts_ref[shard, 6 * tokens : 7 * tokens, :].astype(F32)
        for seq in range(MB):
            for block in range(2):
                segment = span_ref[seq * 2 * shards + shard * 2 + block]
                spot = segment * MB + seq
                piece = seq * 2 + block
                pair = parts_ref[shard, piece * tokens : (piece + 1) * tokens, :]
                third = parts_ref[shard, (4 + block) * tokens : (5 + block) * tokens, :]
                pair_ref[spot] = pair_ref[spot] + pair.astype(F32)
                third_ref[spot] = third_ref[spot] + third.astype(F32)
                sum_ref[spot] = sum_ref[spot] + jnp.where(lane // 32 == piece, sums, 0.0)
    count = shards * tokens
    near = lax.broadcasted_iota(jnp.int32, (count, 2 * HD), 1)
    for seq in range(MB):

        def taken(ref):
            return ref[...].reshape(shards, MB, tokens, 2 * HD)[:, seq].reshape(count, 2 * HD)

        sums = taken(sum_ref)

        def total(head):
            at = 64 * seq + head
            spots = (at, at + heads, at + 32, at + 32 + heads)
            return sum(sums[:, spot : spot + 1] for spot in spots)

        pair = taken(pair_ref) / jnp.where(near < HD, total(0), total(1))
        third = taken(third_ref) / total(2)
        if seq:
            third = pltpu.roll(third, HD, 1)
        third = jnp.where(near < HD, third, 0.0)
        rows = slice(seq * tokens, (seq + 1) * tokens)
        all_ref[:, rows, : 2 * HD] = pair.astype(BF16).reshape(shards, tokens, 2 * HD)
        all_ref[:, rows, 2 * HD :] = third.astype(BF16).reshape(shards, tokens, 2 * HD)
    ctx_ref[...] = all_ref[place_ref[2]][:, : heads * HD]
    context = all_ref[...].reshape(shards * MB * tokens, 4 * HD)
    grad = lax.dot_general(
        cot_ref[...], context, (((0,), (0,)), ((), ())), preferred_element_type=F32
    )
    grad_ref[...] = grad.reshape(grad_ref.shape).astype(BF16)


def columns_kernel(place_ref, cot_ref, out_ref):
    cols = cot_ref.shape[1]
    lanes = out_ref.shape[1]
    each = place_ref[3]
    row = lax.broadcasted_iota(jnp.int32, (cols, lanes), 0)
    lane = lax.broadcasted_iota(jnp.int32, (cols, lanes), 1)
    inside = lane % 16
    hit = (row == (lane // 16) * place_ref[4] + place_ref[2] * each + inside) & (inside < each)
    out_ref[...] = matmul(cot_ref[...], jnp.where(hit, 1.0, 0.0).astype(BF16)).astype(BF16)


def shape(dims, dtype=BF16):
    return jax.ShapeDtypeStruct(dims, dtype)


def per_device(
    frames,
    block_mask,
    span_segment,
    dec_states,
    enc_qkv,
    enc_out,
    cross_query,
    cross_key,
    cross_value,
    cotangent,
):
    sections = lax.axis_size("section")
    shards = lax.axis_size("tm")
    groups = lax.axis_size("dp")
    section = lax.axis_index("section")
    shard = lax.axis_index("tm")
    model = frames.shape[2]
    width = enc_out.shape[1]
    head_width = cross_query.shape[1]
    padded = 256

    def pad_lanes(w):
        return jnp.pad(w, ((0, 0), (0, padded - w.shape[1])))

    def around(value, axis, size, step):
        return lax.ppermute(value, axis, [(i, (i + step) % size) for i in range(size)])

    group = lax.axis_index("dp")
    own = jnp.concatenate([enc_qkv[0], enc_out[0].T], axis=1)
    blocks, steps = [own], [0]
    for step, count in ((1, groups // 2), (-1, (groups - 1) // 2)):
        moving = own
        for hop in range(count):
            moving = around(moving, "dp", groups, step)
            blocks.append(moving)
            steps.append(step * (hop + 1))
    block = jnp.concatenate(blocks, axis=0)
    chips = shards // 2
    ring, source = [block], [shard]
    for step, count in ((2, chips // 2), (-2, (chips - 1) // 2)):
        moving = block
        for hop in range(count):
            moving = around(moving, "tm", shards, step)
            ring.append(moving)
            source.append((shard - step * (hop + 1)) % shards)
    swap = [(i, i ^ 1) for i in range(shards)]
    pieces_w = ring + [lax.ppermute(value, "tm", swap) for value in ring]
    source = jnp.stack(source + [place ^ 1 for place in source])
    each = model // (groups * shards)
    slots = (group - jnp.array(steps)) % groups
    order = (slots[None, :, None] * shards + source[:, None, None]) * each + jnp.arange(each)
    order = order.reshape(-1).astype(jnp.int32)

    cross = jnp.concatenate([pad_lanes(w) for w in (cross_key, cross_value, cross_query)], axis=1)
    cross = lax.all_gather(cross, ("dp", "tm"), axis=0, tiled=True)
    tokens_all = lax.all_gather(
        jnp.concatenate([dec_states, cotangent], axis=1), "tm", axis=0, tiled=True
    )

    place = jnp.stack(
        [
            section,
            jnp.int32(sections - 1),
            shard,
            jnp.int32(each),
            jnp.int32(each * shards),
            jnp.int32(shards - 1),
        ]
    ).astype(jnp.int32)
    mask = block_mask.reshape(-1)
    inputs = pl.pallas_call(
        order_kernel,
        out_shape=(shape(frames.shape[1:]),) * MB,
        in_specs=[VMEM, VMEM],
        out_specs=(VMEM,) * MB,
        compiler_params=PARAMS,
        name="order",
    )(order.reshape(1, -1), frames)

    up = [(i, i + 1) for i in range(shards - 1)]
    down = [(i + 1, i) for i in range(shards - 1)]
    onward = [(i, i + 1) for i in range(sections - 1)]
    rows = frames.shape[1]
    tokens = dec_states.shape[0] // MB
    carried = inputs[0]
    memory = []
    w_q, w_kv, w_out = pl.pallas_call(
        join_kernel,
        out_shape=(shape((model, width)), shape((model, 2 * width)), shape((model, width))),
        in_specs=[pl.BlockSpec(memory_space=pl.ANY)] * len(pieces_w),
        out_specs=(JOINED,) * 3,
        scratch_shapes=[pltpu.SemaphoreType.DMA((3, len(pieces_w)))],
        compiler_params=JOIN_PARAMS,
        name="join",
    )(*pieces_w)
    for moment in range(MB + sections - 1):
        if 0 < moment < MB:
            carried = jnp.where(section == 0, inputs[moment], carried)
        if moment == 2:
            w_cross = pl.pallas_call(
                reorder_kernel,
                grid=(1,),
                out_shape=shape((model, 2 * padded)),
                in_specs=[
                    pl.BlockSpec((model, 1), lambda i: (0, 0)),
                    pl.BlockSpec((model, 2 * padded), lambda i: (0, 0)),
                ],
                out_specs=pl.BlockSpec((model, 2 * padded), lambda i: (0, 0)),
                compiler_params=PARAMS,
                name="reorder",
            )(order.reshape(-1, 1), cross)
            carried, w_cross = lax.optimization_barrier((carried, w_cross))
        if moment == 3:
            mine = lax.dynamic_slice_in_dim(span_segment, shard * 2, 2, axis=1).reshape(-1)
            queries = pl.pallas_call(
                query_kernel,
                grid_spec=pltpu.PrefetchScalarGridSpec(
                    num_scalar_prefetch=1,
                    grid=(4,),
                    in_specs=[
                        pl.BlockSpec((tokens, model), lambda i, seg: (seg[i] * MB + i // 2, 0)),
                        pl.BlockSpec((model, padded), lambda i, seg: (0, 2)),
                    ],
                    out_specs=pl.BlockSpec((tokens, padded), lambda i, seg: (i, 0)),
                ),
                out_shape=shape((4 * tokens, padded)),
                compiler_params=PARAMS,
                name="queries",
            )(mine, tokens_all, cross)
            carried, queries = lax.optimization_barrier((carried, queries))
        if moment == 4:
            cot_cols = pl.pallas_call(
                columns_kernel,
                grid=(1,),
                out_shape=shape((shards * MB * tokens, groups * 16)),
                in_specs=[
                    SMEM,
                    pl.BlockSpec((shards * MB * tokens, model), lambda i: (0, 1)),
                ],
                out_specs=pl.BlockSpec((shards * MB * tokens, groups * 16), lambda i: (0, 0)),
                compiler_params=PARAMS,
                name="columns",
            )(place, tokens_all)
            carried, cot_cols = lax.optimization_barrier((carried, cot_cols))

        n, first, last = pl.pallas_call(
            kv_kernel,
            out_shape=(shape((rows, model)), shape((BLK, 2 * width)), shape((BLK, 2 * width))),
            in_specs=[VMEM, VMEM],
            out_specs=(VMEM, VMEM, VMEM),
            compiler_params=PARAMS,
            name="keys_values",
        )(carried, w_kv)
        left = lax.ppermute(last, "tm", up)
        right = lax.ppermute(first, "tm", down)
        q, num, den = pl.pallas_call(
            functools.partial(own_kernel, moment),
            out_shape=(shape((rows, width)), shape((rows, width), F32), shape((rows, width), F32)),
            in_specs=[SMEM, SMEM] + [VMEM] * 4,
            out_specs=(VMEM, VMEM, VMEM),
            compiler_params=PARAMS,
            name="own_blocks",
        )(place, mask, n, first, last, w_q)
        finished = pl.pallas_call(
            functools.partial(out_kernel, moment),
            out_shape=shape((rows, model)),
            in_specs=[SMEM, SMEM] + [VMEM] * 7,
            out_specs=VMEM,
            scratch_shapes=[pltpu.VMEM((rows, width), BF16)],
            compiler_params=PARAMS,
            name="layer_out",
        )(place, mask, q, num, den, left, right, carried, w_out)
        if moment >= sections - 1:
            memory.append(finished)
            for target in (0, 1, 2):
                memory.append(lax.ppermute(finished, "section", [(sections - 1, target)]))
        if moment < MB + sections - 2:
            carried = lax.ppermute(finished, "section", onward)

    pieces = pl.pallas_call(
        cross_kernel,
        out_shape=shape((7 * tokens, 2 * HD)),
        in_specs=[SMEM] + [VMEM] * 10,
        out_specs=VMEM,
        compiler_params=PARAMS,
        name="cross",
    )(place, queries, w_cross, *memory)
    everyone = lax.all_gather(pieces, "tm", axis=0)
    context, grad = pl.pallas_call(
        combine_kernel,
        out_shape=(
            shape((MB * tokens, head_width)),
            shape((groups, 16, padded)),
        ),
        in_specs=[SMEM, SMEM, VMEM, VMEM],
        out_specs=(VMEM, VMEM),
        scratch_shapes=[pltpu.VMEM((shards * MB, tokens, 2 * HD), F32)] * 3
        + [pltpu.VMEM((shards, MB * tokens, padded), BF16)],
        compiler_params=PARAMS,
        name="combine",
    )(place, span_segment.reshape(-1), everyone, cot_cols)
    grad = lax.all_to_all(grad, "dp", 0, 0, tiled=True)
    grad_shard = jnp.sum(grad.astype(F32), axis=0)[:each, :head_width].T
    return (context, grad_shard)


def solution(mesh):
    in_specs = (
        P("dp", "tm", None),
        P("dp", "tm", None),
        P("dp", None),
        P(("dp", "tm"), None),
        P("section", ("dp", "tm"), None),
        P("section", None, ("dp", "tm")),
        P(("dp", "tm"), "section"),
        P(("dp", "tm"), "section"),
        P(("dp", "tm"), "section"),
        P(("dp", "tm"), None),
    )
    out_specs = (P(("dp", "tm"), "section"), P("section", ("dp", "tm")))
    return jax.shard_map(
        per_device, mesh=mesh, in_specs=in_specs, out_specs=out_specs, check_vma=False
    )
```

```python
import functools

import jax
import jax.numpy as jnp
from jax import lax
from jax.experimental import pallas as pl
from jax.experimental.pallas import tpu as pltpu
from jax.sharding import PartitionSpec as P

HD = 64
BLK = 64
MB = 2
EPS = 1e-05
F32 = jnp.float32
BF16 = jnp.bfloat16
VMEM = pl.BlockSpec(memory_space=pltpu.VMEM)
SMEM = pl.BlockSpec(memory_space=pltpu.SMEM)
PARAMS = pltpu.CompilerParams(vmem_limit_bytes=16 * 1024 * 1024)
JOIN_PARAMS = pltpu.CompilerParams()
JOINED = VMEM


def normed_rows(values):
    wide = values.astype(F32)
    center = wide - jnp.mean(wide, axis=-1, keepdims=True)
    spread = jnp.mean(center * center, axis=-1, keepdims=True)
    return (center * lax.rsqrt(spread + EPS)).astype(BF16)


def matmul(a, b):
    return jnp.dot(a, b, preferred_element_type=F32)


def matmul_nt(a, b):
    return lax.dot_general(a, b, (((1,), (1,)), ((), ())), preferred_element_type=F32)


def join_kernel(*refs):
    pieces, outs, sems = refs[:-4], refs[-4:-1], refs[-1]
    copies = []
    start = 0
    for index, out_ref in enumerate(outs):
        cols = slice(start, start + out_ref.shape[1])
        start += out_ref.shape[1]
        for slot, piece in enumerate(pieces):
            height = piece.shape[0]
            copies.append(
                pltpu.make_async_copy(
                    piece.at[:, cols],
                    out_ref.at[pl.ds(slot * height, height), :],
                    sems.at[index, slot],
                )
            )
    for copy in copies:
        copy.start()
    for copy in copies:
        copy.wait()


def kv_kernel(place_ref, x_ref, w_ref, n_ref, a_ref, b_ref):
    n = normed_rows(x_ref[...])
    n_ref[...] = n
    kv = matmul(n, w_ref[...]).astype(BF16)
    even = place_ref[2] % 2 == 0
    a_ref[...] = jnp.where(even, kv[BLK:], kv[:BLK])
    b_ref[...] = jnp.where(even, kv[:BLK], kv[BLK:])


def allowed_of(moment, halo, place_ref, mask_ref):
    base = 4 * jnp.clip(moment - place_ref[0], 0, MB - 1)
    shard = place_ref[2]
    row = lax.broadcasted_iota(jnp.int32, (4 * BLK, 2 * BLK), 0)
    col = lax.broadcasted_iota(jnp.int32, (4 * BLK, 2 * BLK), 1)
    low_row = (row // BLK) % 2 == 0
    block = jnp.where(shard % 2 == 1, col // BLK, 1 - col // BLK)
    same = (row // BLK) % 2 == block
    if halo:
        before = jnp.where(shard > 0, mask_ref[base], 0)
        after = jnp.where(shard < place_ref[5], mask_ref[base + 3], 0)
        open_side = jnp.where(low_row, before, after) == 1
        return same & open_side
    open_side = jnp.where(low_row, mask_ref[base + 1], mask_ref[base + 2]) == 1
    return same | open_side


def pair_attention(q, k, v, allowed):
    rows = q.shape[0]
    low = lax.broadcasted_iota(jnp.int32, q.shape, 1) < HD
    zero = jnp.zeros_like(q)
    both = jnp.concatenate([jnp.where(low, q, zero), jnp.where(low, zero, q)], axis=0)
    scores = matmul_nt(both, k) * HD ** (-0.5)
    weights = jnp.where(allowed, jnp.exp(scores), 0.0)
    totals = jnp.sum(weights, axis=-1, keepdims=True)
    summed = matmul(weights.astype(BF16), v)
    return (
        jnp.where(low, summed[:rows], summed[rows:]),
        jnp.where(low, totals[:rows], totals[rows:]),
    )


def own_kernel(
    moment, place_ref, mask_ref, n_ref, a_ref, b_ref, w_ref, q_ref, num_ref, den_ref
):
    width = q_ref.shape[1]
    allowed = allowed_of(moment, False, place_ref, mask_ref)
    q = matmul(n_ref[...], w_ref[...]).astype(BF16)
    q_ref[...] = q
    for lane in range(0, width, 2 * HD):
        cols = slice(lane, lane + 2 * HD)
        vcols = slice(width + lane, width + lane + 2 * HD)
        k = jnp.concatenate([a_ref[:, cols], b_ref[:, cols]], axis=0)
        v = jnp.concatenate([a_ref[:, vcols], b_ref[:, vcols]], axis=0)
        num_ref[:, cols], den_ref[:, cols] = pair_attention(q[:, cols], k, v, allowed)


def out_kernel(
    moment, place_ref, mask_ref, q_ref, num_ref, den_ref, a_ref, b_ref, x_ref, w_ref,
    o_ref, ctx_ref
):
    width = q_ref.shape[1]
    allowed = allowed_of(moment, True, place_ref, mask_ref)
    for lane in range(0, width, 2 * HD):
        cols = slice(lane, lane + 2 * HD)
        vcols = slice(width + lane, width + lane + 2 * HD)
        k = jnp.concatenate([a_ref[:, cols], b_ref[:, cols]], axis=0)
        v = jnp.concatenate([a_ref[:, vcols], b_ref[:, vcols]], axis=0)
        num, den = pair_attention(q_ref[:, cols], k, v, allowed)
        ctx_ref[:, cols] = ((num + num_ref[:, cols]) / (den + den_ref[:, cols])).astype(BF16)
    update = matmul_nt(ctx_ref[...], w_ref[...])
    o_ref[...] = (x_ref[...].astype(F32) + update).astype(BF16)


def order_kernel(order_ref, frames_ref, *out_refs):
    seqs, rows, model = frames_ref.shape
    frames = frames_ref[...].reshape(seqs * rows, model)
    for lane in range(0, model, 256):
        source = lax.broadcasted_iota(jnp.int32, (model, 256), 0)
        hit = source == order_ref[:, lane : lane + 256]
        pick = jnp.where(hit, 1.0, 0.0).astype(BF16)
        moved = matmul(frames, pick).astype(BF16)
        for seq, out_ref in enumerate(out_refs):
            out_ref[:, lane : lane + 256] = moved[seq * rows : (seq + 1) * rows]


def reorder_kernel(order_ref, w_ref, out_ref):
    model = w_ref.shape[0]
    for row in range(0, model, 256):
        source = lax.broadcasted_iota(jnp.int32, (256, model), 1)
        hit = source == order_ref[row : row + 256, :]
        pick = jnp.where(hit, 1.0, 0.0).astype(BF16)
        out_ref[row : row + 256, :] = matmul(pick, w_ref[...]).astype(BF16)


def query_kernel(seg_ref, dec_ref, w_ref, q_ref):
    q_ref[...] = matmul(normed_rows(dec_ref[...]), w_ref[...]).astype(BF16)


def cross_kernel(place_ref, q_ref, w_ref, *refs):
    parts, out_ref = refs[:-1], refs[-1]
    owner = place_ref[0] == place_ref[1]
    rows = []
    for start in (0, 4):
        own, a, b, c = (ref[...] for ref in parts[start : start + 4])
        rows.append(jnp.where(owner, own, a + b + c))
    n = normed_rows(jnp.concatenate(rows, axis=0))
    width = q_ref.shape[1]
    both = matmul(n, w_ref[...]).astype(BF16)
    keys, values = both[:, :width], both[:, width:]
    tokens = q_ref.shape[0] // 4
    heads = 3
    lane = lax.broadcasted_iota(jnp.int32, (tokens, width), 1)
    near = lax.broadcasted_iota(jnp.int32, (tokens, 2 * HD), 1)
    sums = jnp.zeros((tokens, 2 * HD), F32)
    thirds = []
    for piece in range(4):
        q = q_ref[piece * tokens : (piece + 1) * tokens, :]
        spots = slice(piece * BLK, (piece + 1) * BLK)
        stacked = jnp.concatenate(
            [jnp.where(lane // HD == head, q, jnp.zeros_like(q)) for head in range(heads)], axis=0
        )
        weights = jnp.exp(matmul_nt(stacked, keys[spots]) * HD ** (-0.5))
        totals = jnp.sum(weights, axis=-1, keepdims=True)
        summed = matmul(weights.astype(BF16), values[spots])
        high = totals.astype(BF16).astype(F32)
        rest = totals - high
        for head in range(heads):
            mine = slice(head * tokens, (head + 1) * tokens)
            sums = jnp.where(near == 32 * piece + head, high[mine], sums)
            sums = jnp.where(near == 32 * piece + heads + head, rest[mine], sums)
        pair = jnp.where(near < HD, summed[:tokens, : 2 * HD], summed[tokens : 2 * tokens, : 2 * HD])
        out_ref[piece * tokens : (piece + 1) * tokens, :] = pair.astype(BF16)
        thirds.append(summed[2 * tokens :, 2 * HD :])
    at = 4 * tokens
    for block in range(2):
        shifted = pltpu.roll(thirds[2 + block], HD, 1)
        out_ref[at + block * tokens : at + (block + 1) * tokens, :] = jnp.where(
            near < HD, thirds[block], shifted
        ).astype(BF16)
    out_ref[at + 2 * tokens :, :] = sums.astype(BF16)


def combine_kernel(
    place_ref, span_ref, parts_ref, cot_ref, ctx_ref, grad_ref, pair_ref, third_ref, sum_ref, all_ref
):
    shards = parts_ref.shape[0]
    tokens = pair_ref.shape[1]
    heads = 3
    for ref in (pair_ref, third_ref, sum_ref):
        ref[...] = jnp.zeros_like(ref)
    lane = lax.broadcasted_iota(jnp.int32, (tokens, 2 * HD), 1)
    for shard in range(shards):
        sums = parts_ref[shard, 6 * tokens : 7 * tokens, :].astype(F32)
        for seq in range(MB):
            for block in range(2):
                segment = span_ref[seq * 2 * shards + shard * 2 + block]
                spot = segment * MB + seq
                piece = seq * 2 + block
                pair = parts_ref[shard, piece * tokens : (piece + 1) * tokens, :]
                third = parts_ref[shard, (4 + block) * tokens : (5 + block) * tokens, :]
                pair_ref[spot] = pair_ref[spot] + pair.astype(F32)
                third_ref[spot] = third_ref[spot] + third.astype(F32)
                sum_ref[spot] = sum_ref[spot] + jnp.where(lane // 32 == piece, sums, 0.0)
    count = shards * tokens
    near = lax.broadcasted_iota(jnp.int32, (count, 2 * HD), 1)
    for seq in range(MB):

        def taken(ref):
            return ref[...].reshape(shards, MB, tokens, 2 * HD)[:, seq].reshape(count, 2 * HD)

        sums = taken(sum_ref)

        def total(head):
            at = 64 * seq + head
            spots = (at, at + heads, at + 32, at + 32 + heads)
            return sum(sums[:, spot : spot + 1] for spot in spots)

        pair = taken(pair_ref) / jnp.where(near < HD, total(0), total(1))
        third = taken(third_ref) / total(2)
        if seq:
            third = pltpu.roll(third, HD, 1)
        third = jnp.where(near < HD, third, 0.0)
        rows = slice(seq * tokens, (seq + 1) * tokens)
        all_ref[:, rows, : 2 * HD] = pair.astype(BF16).reshape(shards, tokens, 2 * HD)
        all_ref[:, rows, 2 * HD :] = third.astype(BF16).reshape(shards, tokens, 2 * HD)
    ctx_ref[...] = all_ref[place_ref[2]][:, : heads * HD]
    context = all_ref[...].reshape(shards * MB * tokens, 4 * HD)
    grad = lax.dot_general(
        cot_ref[...], context, (((0,), (0,)), ((), ())), preferred_element_type=F32
    )
    grad_ref[...] = grad.reshape(grad_ref.shape).astype(BF16)


def columns_kernel(place_ref, cot_ref, out_ref):
    cols = cot_ref.shape[1]
    lanes = out_ref.shape[1]
    each = place_ref[3]
    row = lax.broadcasted_iota(jnp.int32, (cols, lanes), 0)
    lane = lax.broadcasted_iota(jnp.int32, (cols, lanes), 1)
    inside = lane % 16
    hit = (row == (lane // 16) * place_ref[4] + place_ref[2] * each + inside) & (inside < each)
    out_ref[...] = matmul(cot_ref[...], jnp.where(hit, 1.0, 0.0).astype(BF16)).astype(BF16)


def shape(dims, dtype=BF16):
    return jax.ShapeDtypeStruct(dims, dtype)


def per_device(
    frames,
    block_mask,
    span_segment,
    dec_states,
    enc_qkv,
    enc_out,
    cross_query,
    cross_key,
    cross_value,
    cotangent,
):
    sections = lax.axis_size("section")
    shards = lax.axis_size("tm")
    groups = lax.axis_size("dp")
    section = lax.axis_index("section")
    shard = lax.axis_index("tm")
    model = frames.shape[2]
    width = enc_out.shape[1]
    head_width = cross_query.shape[1]
    padded = 256

    def pad_lanes(w):
        return jnp.pad(w, ((0, 0), (0, padded - w.shape[1])))

    def around(value, axis, size, step):
        return lax.ppermute(value, axis, [(i, (i + step) % size) for i in range(size)])

    group = lax.axis_index("dp")
    own = jnp.concatenate([enc_qkv[0], enc_out[0].T], axis=1)
    def pairs(size, wrap):
        even = [(i, i ^ 1) for i in range(size)]
        odd = [(i, i - 1 if i % 2 == 0 else i + 1) for i in range(size)]
        if wrap:
            return even, [(i, j % size) for i, j in odd]
        return even, [(i, j) for i, j in odd if 0 <= j < size]

    swaps = pairs(groups, True)
    first = lax.ppermute(own, "dp", swaps[0])
    blocks, steps = [own, first], [0, 1]
    moving = jnp.stack([own, first])
    for turn in range(2, groups // 2 + 1):
        moving = lax.ppermute(moving, "dp", swaps[(turn - 1) % 2])
        blocks += [moving[0], moving[1]]
        sign = 1 if turn % 2 else -1
        steps += [sign * (turn - 1), sign * turn]
    block = jnp.concatenate(blocks, axis=0)
    chips = shards // 2
    ring, source = [block], [shard]
    for step, count in ((2, chips // 2), (-2, (chips - 1) // 2)):
        moving = block
        for hop in range(count):
            moving = around(moving, "tm", shards, step)
            ring.append(moving)
            source.append((shard - step * (hop + 1)) % shards)
    swap = [(i, i ^ 1) for i in range(shards)]
    pieces_w = ring + [lax.ppermute(value, "tm", swap) for value in ring]
    source = jnp.stack(source + [place ^ 1 for place in source])
    each = model // (groups * shards)
    side = 1 - 2 * (group % 2)
    slots = (group + side * jnp.array(steps)) % groups
    order = (slots[None, :, None] * shards + source[:, None, None]) * each + jnp.arange(each)
    order = order.reshape(-1).astype(jnp.int32)

    cross = jnp.concatenate([pad_lanes(w) for w in (cross_key, cross_value, cross_query)], axis=1)
    cross = lax.all_gather(cross, ("dp", "tm"), axis=0, tiled=True)
    tokens_all = lax.all_gather(
        jnp.concatenate([dec_states, cotangent], axis=1), "tm", axis=0, tiled=True
    )

    place = jnp.stack(
        [
            section,
            jnp.int32(sections - 1),
            shard,
            jnp.int32(each),
            jnp.int32(each * shards),
            jnp.int32(shards - 1),
        ]
    ).astype(jnp.int32)
    mask = block_mask.reshape(-1)
    inputs = pl.pallas_call(
        order_kernel,
        out_shape=(shape(frames.shape[1:]),) * MB,
        in_specs=[VMEM, VMEM],
        out_specs=(VMEM,) * MB,
        compiler_params=PARAMS,
        name="order",
    )(order.reshape(1, -1), frames)

    halos = pairs(shards, False)
    onward = [(i, i + 1) for i in range(sections - 1)]
    rows = frames.shape[1]
    tokens = dec_states.shape[0] // MB
    carried = inputs[0]
    memory = []
    w_q, w_kv, w_out = pl.pallas_call(
        join_kernel,
        out_shape=(shape((model, width)), shape((model, 2 * width)), shape((model, width))),
        in_specs=[pl.BlockSpec(memory_space=pl.ANY)] * len(pieces_w),
        out_specs=(JOINED,) * 3,
        scratch_shapes=[pltpu.SemaphoreType.DMA((3, len(pieces_w)))],
        compiler_params=JOIN_PARAMS,
        name="join",
    )(*pieces_w)
    for moment in range(MB + sections - 1):
        if moment == 1:
            carried, cross = lax.optimization_barrier((carried, cross))
        if 0 < moment < MB:
            carried = jnp.where(section == 0, inputs[moment], carried)
        if moment == 2:
            w_cross = pl.pallas_call(
                reorder_kernel,
                grid=(1,),
                out_shape=shape((model, 2 * padded)),
                in_specs=[
                    pl.BlockSpec((model, 1), lambda i: (0, 0)),
                    pl.BlockSpec((model, 2 * padded), lambda i: (0, 0)),
                ],
                out_specs=pl.BlockSpec((model, 2 * padded), lambda i: (0, 0)),
                compiler_params=PARAMS,
                name="reorder",
            )(order.reshape(-1, 1), cross)
            carried, w_cross = lax.optimization_barrier((carried, w_cross))
        if moment == 3:
            mine = lax.dynamic_slice_in_dim(span_segment, shard * 2, 2, axis=1).reshape(-1)
            queries = pl.pallas_call(
                query_kernel,
                grid_spec=pltpu.PrefetchScalarGridSpec(
                    num_scalar_prefetch=1,
                    grid=(4,),
                    in_specs=[
                        pl.BlockSpec((tokens, model), lambda i, seg: (seg[i] * MB + i // 2, 0)),
                        pl.BlockSpec((model, padded), lambda i, seg: (0, 2)),
                    ],
                    out_specs=pl.BlockSpec((tokens, padded), lambda i, seg: (i, 0)),
                ),
                out_shape=shape((4 * tokens, padded)),
                compiler_params=PARAMS,
                name="queries",
            )(mine, tokens_all, cross)
            carried, queries = lax.optimization_barrier((carried, queries))
        if moment == 4:
            cot_cols = pl.pallas_call(
                columns_kernel,
                grid=(1,),
                out_shape=shape((shards * MB * tokens, groups * 16)),
                in_specs=[
                    SMEM,
                    pl.BlockSpec((shards * MB * tokens, model), lambda i: (0, 1)),
                ],
                out_specs=pl.BlockSpec((shards * MB * tokens, groups * 16), lambda i: (0, 0)),
                compiler_params=PARAMS,
                name="columns",
            )(place, tokens_all)
            carried, cot_cols = lax.optimization_barrier((carried, cot_cols))

        n, near, far = pl.pallas_call(
            kv_kernel,
            out_shape=(shape((rows, model)), shape((BLK, 2 * width)), shape((BLK, 2 * width))),
            in_specs=[SMEM, VMEM, VMEM],
            out_specs=(VMEM, VMEM, VMEM),
            compiler_params=PARAMS,
            name="keys_values",
        )(place, carried, w_kv)
        from_near = lax.ppermute(near, "tm", halos[0])
        from_far = lax.ppermute(far, "tm", halos[1])
        q, num, den = pl.pallas_call(
            functools.partial(own_kernel, moment),
            out_shape=(shape((rows, width)), shape((rows, width), F32), shape((rows, width), F32)),
            in_specs=[SMEM, SMEM] + [VMEM] * 4,
            out_specs=(VMEM, VMEM, VMEM),
            compiler_params=PARAMS,
            name="own_blocks",
        )(place, mask, n, near, far, w_q)
        finished = pl.pallas_call(
            functools.partial(out_kernel, moment),
            out_shape=shape((rows, model)),
            in_specs=[SMEM, SMEM] + [VMEM] * 7,
            out_specs=VMEM,
            scratch_shapes=[pltpu.VMEM((rows, width), BF16)],
            compiler_params=PARAMS,
            name="layer_out",
        )(place, mask, q, num, den, from_near, from_far, carried, w_out)
        if moment >= sections - 1:
            memory.append(finished)
            for target in (0, 1, 2):
                memory.append(lax.ppermute(finished, "section", [(sections - 1, target)]))
        if moment < MB + sections - 2:
            carried = lax.ppermute(finished, "section", onward)

    pieces = pl.pallas_call(
        cross_kernel,
        out_shape=shape((7 * tokens, 2 * HD)),
        in_specs=[SMEM] + [VMEM] * 10,
        out_specs=VMEM,
        compiler_params=PARAMS,
        name="cross",
    )(place, queries, w_cross, *memory)
    everyone = lax.all_gather(pieces, "tm", axis=0)
    context, grad = pl.pallas_call(
        combine_kernel,
        out_shape=(
            shape((MB * tokens, head_width)),
            shape((groups, 16, padded)),
        ),
        in_specs=[SMEM, SMEM, VMEM, VMEM],
        out_specs=(VMEM, VMEM),
        scratch_shapes=[pltpu.VMEM((shards * MB, tokens, 2 * HD), F32)] * 3
        + [pltpu.VMEM((shards, MB * tokens, padded), BF16)],
        compiler_params=PARAMS,
        name="combine",
    )(place, span_segment.reshape(-1), everyone, cot_cols)
    grad = lax.all_to_all(grad, "dp", 0, 0, tiled=True)
    grad_shard = jnp.sum(grad.astype(F32), axis=0)[:each, :head_width].T
    return (context, grad_shard)


def solution(mesh):
    in_specs = (
        P("dp", "tm", None),
        P("dp", "tm", None),
        P("dp", None),
        P(("dp", "tm"), None),
        P("section", ("dp", "tm"), None),
        P("section", None, ("dp", "tm")),
        P(("dp", "tm"), "section"),
        P(("dp", "tm"), "section"),
        P(("dp", "tm"), "section"),
        P(("dp", "tm"), None),
    )
    out_specs = (P(("dp", "tm"), "section"), P("section", ("dp", "tm")))
    return jax.shard_map(
        per_device, mesh=mesh, in_specs=in_specs, out_specs=out_specs, check_vma=False
    )
```

```python
import functools

import jax
import jax.numpy as jnp
from jax import lax
from jax.experimental import pallas as pl
from jax.experimental.pallas import tpu as pltpu
from jax.sharding import PartitionSpec as P

HD = 64
BLK = 64
MB = 2
EPS = 1e-05
F32 = jnp.float32
BF16 = jnp.bfloat16
VMEM = pl.BlockSpec(memory_space=pltpu.VMEM)
SMEM = pl.BlockSpec(memory_space=pltpu.SMEM)
PARAMS = pltpu.CompilerParams(vmem_limit_bytes=16 * 1024 * 1024)


def normed_rows(values):
    wide = values.astype(F32)
    center = wide - jnp.mean(wide, axis=-1, keepdims=True)
    spread = jnp.mean(center * center, axis=-1, keepdims=True)
    return (center * lax.rsqrt(spread + EPS)).astype(BF16)


def matmul(a, b):
    return jnp.dot(a, b, preferred_element_type=F32)


def matmul_nt(a, b):
    return lax.dot_general(a, b, (((1,), (1,)), ((), ())), preferred_element_type=F32)


def join_kernel(*refs):
    pieces, outs, sems = refs[:-4], refs[-4:-1], refs[-1]
    copies = []
    start = 0
    for index, out_ref in enumerate(outs):
        cols = slice(start, start + out_ref.shape[1])
        start += out_ref.shape[1]
        for slot, piece in enumerate(pieces):
            height = piece.shape[0]
            copies.append(
                pltpu.make_async_copy(
                    piece.at[:, cols],
                    out_ref.at[pl.ds(slot * height, height), :],
                    sems.at[index, slot],
                )
            )
    for copy in copies:
        copy.start()
    for copy in copies:
        copy.wait()


def halves_product(n, near_ref, far_ref):
    half = near_ref.shape[0]
    return matmul(n[:, :half], near_ref[...]) + matmul(n[:, half:], far_ref[...])


def kv_kernel(x_ref, near_ref, far_ref, n_ref, first_ref, last_ref):
    n = normed_rows(x_ref[...])
    n_ref[...] = n
    kv = halves_product(n, near_ref, far_ref).astype(BF16)
    first_ref[...] = kv[:BLK]
    last_ref[...] = kv[BLK:]


def allowed_of(moment, halo, place_ref, mask_ref):
    base = 4 * jnp.clip(moment - place_ref[0], 0, MB - 1)
    shard = place_ref[2]
    row = lax.broadcasted_iota(jnp.int32, (4 * BLK, 2 * BLK), 0)
    col = lax.broadcasted_iota(jnp.int32, (4 * BLK, 2 * BLK), 1)
    same = ((row // BLK) % 2 == 0) == (col < BLK)
    low_row = (row // BLK) % 2 == 0
    if halo:
        before = jnp.where(shard > 0, mask_ref[base], 0)
        after = jnp.where(shard < place_ref[5], mask_ref[base + 3], 0)
        open_side = jnp.where(low_row, before, after) == 1
        return same & open_side
    open_side = jnp.where(low_row, mask_ref[base + 1], mask_ref[base + 2]) == 1
    return same | open_side


def pair_attention(q, k, v, allowed):
    rows = q.shape[0]
    low = lax.broadcasted_iota(jnp.int32, q.shape, 1) < HD
    zero = jnp.zeros_like(q)
    both = jnp.concatenate([jnp.where(low, q, zero), jnp.where(low, zero, q)], axis=0)
    scores = matmul_nt(both, k) * HD ** (-0.5)
    weights = jnp.where(allowed, jnp.exp(scores), 0.0)
    totals = jnp.sum(weights, axis=-1, keepdims=True)
    summed = matmul(weights.astype(BF16), v)
    return (
        jnp.where(low, summed[:rows], summed[rows:]),
        jnp.where(low, totals[:rows], totals[rows:]),
    )


def own_kernel(
    moment, place_ref, mask_ref, n_ref, first_ref, last_ref, near_ref, far_ref, q_ref, num_ref, den_ref
):
    width = q_ref.shape[1]
    allowed = allowed_of(moment, False, place_ref, mask_ref)
    q = halves_product(n_ref[...], near_ref, far_ref).astype(BF16)
    q_ref[...] = q
    for lane in range(0, width, 2 * HD):
        cols = slice(lane, lane + 2 * HD)
        vcols = slice(width + lane, width + lane + 2 * HD)
        k = jnp.concatenate([first_ref[:, cols], last_ref[:, cols]], axis=0)
        v = jnp.concatenate([first_ref[:, vcols], last_ref[:, vcols]], axis=0)
        num_ref[:, cols], den_ref[:, cols] = pair_attention(q[:, cols], k, v, allowed)


def out_kernel(
    moment, place_ref, mask_ref, q_ref, num_ref, den_ref, left_ref, right_ref, x_ref, near_ref, far_ref,
    o_ref, ctx_ref
):
    width = q_ref.shape[1]
    allowed = allowed_of(moment, True, place_ref, mask_ref)
    for lane in range(0, width, 2 * HD):
        cols = slice(lane, lane + 2 * HD)
        vcols = slice(width + lane, width + lane + 2 * HD)
        k = jnp.concatenate([left_ref[:, cols], right_ref[:, cols]], axis=0)
        v = jnp.concatenate([left_ref[:, vcols], right_ref[:, vcols]], axis=0)
        num, den = pair_attention(q_ref[:, cols], k, v, allowed)
        ctx_ref[:, cols] = ((num + num_ref[:, cols]) / (den + den_ref[:, cols])).astype(BF16)
    half = near_ref.shape[0]
    for cols, w_ref in ((slice(0, half), near_ref), (slice(half, 2 * half), far_ref)):
        update = matmul_nt(ctx_ref[...], w_ref[...])
        o_ref[:, cols] = (x_ref[:, cols].astype(F32) + update).astype(BF16)


def order_kernel(order_ref, frames_ref, *out_refs):
    seqs, rows, model = frames_ref.shape
    frames = frames_ref[...].reshape(seqs * rows, model)
    for lane in range(0, model, 256):
        source = lax.broadcasted_iota(jnp.int32, (model, 256), 0)
        hit = source == order_ref[:, lane : lane + 256]
        pick = jnp.where(hit, 1.0, 0.0).astype(BF16)
        moved = matmul(frames, pick).astype(BF16)
        for seq, out_ref in enumerate(out_refs):
            out_ref[:, lane : lane + 256] = moved[seq * rows : (seq + 1) * rows]


def reorder_kernel(order_ref, w_ref, out_ref):
    model = w_ref.shape[0]
    for row in range(0, model, 256):
        source = lax.broadcasted_iota(jnp.int32, (256, model), 1)
        hit = source == order_ref[row : row + 256, :]
        pick = jnp.where(hit, 1.0, 0.0).astype(BF16)
        out_ref[row : row + 256, :] = matmul(pick, w_ref[...]).astype(BF16)


def query_kernel(seg_ref, dec_ref, w_ref, q_ref):
    q_ref[...] = matmul(normed_rows(dec_ref[...]), w_ref[...]).astype(BF16)


def cross_kernel(place_ref, q_ref, w_ref, *refs):
    parts, out_ref = refs[:-1], refs[-1]
    owner = place_ref[0] == place_ref[1]
    rows = []
    for start in (0, 4):
        own, a, b, c = (ref[...] for ref in parts[start : start + 4])
        rows.append(jnp.where(owner, own, a + b + c))
    n = normed_rows(jnp.concatenate(rows, axis=0))
    width = q_ref.shape[1]
    both = matmul(n, w_ref[...]).astype(BF16)
    keys, values = both[:, :width], both[:, width:]
    tokens = q_ref.shape[0] // 4
    heads = 3
    lane = lax.broadcasted_iota(jnp.int32, (tokens, width), 1)
    near = lax.broadcasted_iota(jnp.int32, (tokens, 2 * HD), 1)
    sums = jnp.zeros((tokens, 2 * HD), F32)
    thirds = []
    for piece in range(4):
        q = q_ref[piece * tokens : (piece + 1) * tokens, :]
        spots = slice(piece * BLK, (piece + 1) * BLK)
        stacked = jnp.concatenate(
            [jnp.where(lane // HD == head, q, jnp.zeros_like(q)) for head in range(heads)], axis=0
        )
        weights = jnp.exp(matmul_nt(stacked, keys[spots]) * HD ** (-0.5))
        totals = jnp.sum(weights, axis=-1, keepdims=True)
        summed = matmul(weights.astype(BF16), values[spots])
        high = totals.astype(BF16).astype(F32)
        rest = totals - high
        for head in range(heads):
            mine = slice(head * tokens, (head + 1) * tokens)
            sums = jnp.where(near == 32 * piece + head, high[mine], sums)
            sums = jnp.where(near == 32 * piece + heads + head, rest[mine], sums)
        pair = jnp.where(near < HD, summed[:tokens, : 2 * HD], summed[tokens : 2 * tokens, : 2 * HD])
        out_ref[piece * tokens : (piece + 1) * tokens, :] = pair.astype(BF16)
        thirds.append(summed[2 * tokens :, 2 * HD :])
    at = 4 * tokens
    for block in range(2):
        shifted = pltpu.roll(thirds[2 + block], HD, 1)
        out_ref[at + block * tokens : at + (block + 1) * tokens, :] = jnp.where(
            near < HD, thirds[block], shifted
        ).astype(BF16)
    out_ref[at + 2 * tokens :, :] = sums.astype(BF16)


def combine_kernel(
    place_ref, span_ref, parts_ref, cot_ref, ctx_ref, grad_ref, pair_ref, third_ref, sum_ref, all_ref
):
    shards = parts_ref.shape[0]
    tokens = pair_ref.shape[1]
    heads = 3
    for ref in (pair_ref, third_ref, sum_ref):
        ref[...] = jnp.zeros_like(ref)
    lane = lax.broadcasted_iota(jnp.int32, (tokens, 2 * HD), 1)
    for shard in range(shards):
        sums = parts_ref[shard, 6 * tokens : 7 * tokens, :].astype(F32)
        for seq in range(MB):
            for block in range(2):
                segment = span_ref[seq * 2 * shards + shard * 2 + block]
                spot = segment * MB + seq
                piece = seq * 2 + block
                pair = parts_ref[shard, piece * tokens : (piece + 1) * tokens, :]
                third = parts_ref[shard, (4 + block) * tokens : (5 + block) * tokens, :]
                pair_ref[spot] = pair_ref[spot] + pair.astype(F32)
                third_ref[spot] = third_ref[spot] + third.astype(F32)
                sum_ref[spot] = sum_ref[spot] + jnp.where(lane // 32 == piece, sums, 0.0)
    count = shards * tokens
    near = lax.broadcasted_iota(jnp.int32, (count, 2 * HD), 1)
    for seq in range(MB):

        def taken(ref):
            return ref[...].reshape(shards, MB, tokens, 2 * HD)[:, seq].reshape(count, 2 * HD)

        sums = taken(sum_ref)

        def total(head):
            at = 64 * seq + head
            spots = (at, at + heads, at + 32, at + 32 + heads)
            return sum(sums[:, spot : spot + 1] for spot in spots)

        pair = taken(pair_ref) / jnp.where(near < HD, total(0), total(1))
        third = taken(third_ref) / total(2)
        if seq:
            third = pltpu.roll(third, HD, 1)
        third = jnp.where(near < HD, third, 0.0)
        rows = slice(seq * tokens, (seq + 1) * tokens)
        all_ref[:, rows, : 2 * HD] = pair.astype(BF16).reshape(shards, tokens, 2 * HD)
        all_ref[:, rows, 2 * HD :] = third.astype(BF16).reshape(shards, tokens, 2 * HD)
    ctx_ref[...] = all_ref[place_ref[2]][:, : heads * HD]
    context = all_ref[...].reshape(shards * MB * tokens, 4 * HD)
    grad = lax.dot_general(
        cot_ref[...], context, (((0,), (0,)), ((), ())), preferred_element_type=F32
    )
    grad_ref[...] = grad.reshape(grad_ref.shape).astype(BF16)


def columns_kernel(place_ref, cot_ref, out_ref):
    cols = cot_ref.shape[1]
    lanes = out_ref.shape[1]
    each = place_ref[3]
    row = lax.broadcasted_iota(jnp.int32, (cols, lanes), 0)
    lane = lax.broadcasted_iota(jnp.int32, (cols, lanes), 1)
    inside = lane % 16
    hit = (row == (lane // 16) * place_ref[4] + place_ref[2] * each + inside) & (inside < each)
    out_ref[...] = matmul(cot_ref[...], jnp.where(hit, 1.0, 0.0).astype(BF16)).astype(BF16)


def shape(dims, dtype=BF16):
    return jax.ShapeDtypeStruct(dims, dtype)


def per_device(
    frames,
    block_mask,
    span_segment,
    dec_states,
    enc_qkv,
    enc_out,
    cross_query,
    cross_key,
    cross_value,
    cotangent,
):
    sections = lax.axis_size("section")
    shards = lax.axis_size("tm")
    groups = lax.axis_size("dp")
    section = lax.axis_index("section")
    shard = lax.axis_index("tm")
    model = frames.shape[2]
    width = enc_out.shape[1]
    head_width = cross_query.shape[1]
    padded = 256

    def pad_lanes(w):
        return jnp.pad(w, ((0, 0), (0, padded - w.shape[1])))

    def around(value, axis, size, step):
        return lax.ppermute(value, axis, [(i, (i + step) % size) for i in range(size)])

    group = lax.axis_index("dp")
    own = jnp.concatenate([enc_qkv[0], enc_out[0].T], axis=1)
    blocks, steps = [own], [0]
    for step, count in ((1, groups // 2), (-1, (groups - 1) // 2)):
        moving = own
        for hop in range(count):
            moving = around(moving, "dp", groups, step)
            blocks.append(moving)
            steps.append(step * (hop + 1))
    block = jnp.concatenate(blocks, axis=0)
    chips = shards // 2
    ring, source = [block], [shard]
    for step, count in ((2, chips // 2), (-2, (chips - 1) // 2)):
        moving = block
        for hop in range(count):
            moving = around(moving, "tm", shards, step)
            ring.append(moving)
            source.append((shard - step * (hop + 1)) % shards)
    swap = [(i, i ^ 1) for i in range(shards)]
    source = jnp.stack(source + [place ^ 1 for place in source])
    each = model // (groups * shards)
    slots = (group - jnp.array(steps)) % groups
    order = (slots[None, :, None] * shards + source[:, None, None]) * each + jnp.arange(each)
    order = order.reshape(-1).astype(jnp.int32)

    half = model // 2
    q_near, kv_near, out_near = pl.pallas_call(
        join_kernel,
        out_shape=(shape((half, width)), shape((half, 2 * width)), shape((half, width))),
        in_specs=[pl.BlockSpec(memory_space=pl.ANY)] * len(ring),
        out_specs=(VMEM,) * 3,
        scratch_shapes=[pltpu.SemaphoreType.DMA((3, len(ring)))],
        compiler_params=pltpu.CompilerParams(),
        name="join",
    )(*ring)
    swap = [(i, i ^ 1) for i in range(shards)]
    kv_far, q_far, out_far = (lax.ppermute(w, "tm", swap) for w in (kv_near, q_near, out_near))

    cross = jnp.concatenate([pad_lanes(w) for w in (cross_key, cross_value, cross_query)], axis=1)
    cross = lax.all_gather(cross, ("dp", "tm"), axis=0, tiled=True)
    tokens_all = lax.all_gather(
        jnp.concatenate([dec_states, cotangent], axis=1), "tm", axis=0, tiled=True
    )

    place = jnp.stack(
        [
            section,
            jnp.int32(sections - 1),
            shard,
            jnp.int32(each),
            jnp.int32(each * shards),
            jnp.int32(shards - 1),
        ]
    ).astype(jnp.int32)
    mask = block_mask.reshape(-1)
    inputs = pl.pallas_call(
        order_kernel,
        out_shape=(shape(frames.shape[1:]),) * MB,
        in_specs=[VMEM, VMEM],
        out_specs=(VMEM,) * MB,
        compiler_params=PARAMS,
        name="order",
    )(order.reshape(1, -1), frames)

    up = [(i, i + 1) for i in range(shards - 1)]
    down = [(i + 1, i) for i in range(shards - 1)]
    onward = [(i, i + 1) for i in range(sections - 1)]
    rows = frames.shape[1]
    tokens = dec_states.shape[0] // MB
    carried = inputs[0]
    memory = []
    for moment in range(MB + sections - 1):
        if moment == 1:
            carried, cross = lax.optimization_barrier((carried, cross))
        if 0 < moment < MB:
            carried = jnp.where(section == 0, inputs[moment], carried)
        if moment == 2:
            w_cross = pl.pallas_call(
                reorder_kernel,
                grid=(1,),
                out_shape=shape((model, 2 * padded)),
                in_specs=[
                    pl.BlockSpec((model, 1), lambda i: (0, 0)),
                    pl.BlockSpec((model, 2 * padded), lambda i: (0, 0)),
                ],
                out_specs=pl.BlockSpec((model, 2 * padded), lambda i: (0, 0)),
                compiler_params=PARAMS,
                name="reorder",
            )(order.reshape(-1, 1), cross)
            carried, w_cross = lax.optimization_barrier((carried, w_cross))
        if moment == 3:
            mine = lax.dynamic_slice_in_dim(span_segment, shard * 2, 2, axis=1).reshape(-1)
            queries = pl.pallas_call(
                query_kernel,
                grid_spec=pltpu.PrefetchScalarGridSpec(
                    num_scalar_prefetch=1,
                    grid=(4,),
                    in_specs=[
                        pl.BlockSpec((tokens, model), lambda i, seg: (seg[i] * MB + i // 2, 0)),
                        pl.BlockSpec((model, padded), lambda i, seg: (0, 2)),
                    ],
                    out_specs=pl.BlockSpec((tokens, padded), lambda i, seg: (i, 0)),
                ),
                out_shape=shape((4 * tokens, padded)),
                compiler_params=PARAMS,
                name="queries",
            )(mine, tokens_all, cross)
            carried, queries = lax.optimization_barrier((carried, queries))
        if moment == 4:
            cot_cols = pl.pallas_call(
                columns_kernel,
                grid=(1,),
                out_shape=shape((shards * MB * tokens, groups * 16)),
                in_specs=[
                    SMEM,
                    pl.BlockSpec((shards * MB * tokens, model), lambda i: (0, 1)),
                ],
                out_specs=pl.BlockSpec((shards * MB * tokens, groups * 16), lambda i: (0, 0)),
                compiler_params=PARAMS,
                name="columns",
            )(place, tokens_all)
            carried, cot_cols = lax.optimization_barrier((carried, cot_cols))

        n, first, last = pl.pallas_call(
            kv_kernel,
            out_shape=(shape((rows, model)), shape((BLK, 2 * width)), shape((BLK, 2 * width))),
            in_specs=[VMEM] * 3,
            out_specs=(VMEM, VMEM, VMEM),
            compiler_params=PARAMS,
            name="keys_values",
        )(carried, kv_near, kv_far)
        left = lax.ppermute(last, "tm", up)
        right = lax.ppermute(first, "tm", down)
        q, num, den = pl.pallas_call(
            functools.partial(own_kernel, moment),
            out_shape=(shape((rows, width)), shape((rows, width), F32), shape((rows, width), F32)),
            in_specs=[SMEM, SMEM] + [VMEM] * 5,
            out_specs=(VMEM, VMEM, VMEM),
            compiler_params=PARAMS,
            name="own_blocks",
        )(place, mask, n, first, last, q_near, q_far)
        if moment == sections:
            q, relayed = lax.optimization_barrier((q, relayed))
            memory.append(lax.ppermute(relayed, "section", [(0, 1)]))
        finished = pl.pallas_call(
            functools.partial(out_kernel, moment),
            out_shape=shape((rows, model)),
            in_specs=[SMEM, SMEM] + [VMEM] * 8,
            out_specs=VMEM,
            scratch_shapes=[pltpu.VMEM((rows, width), BF16)],
            compiler_params=PARAMS,
            name="layer_out",
        )(place, mask, q, num, den, left, right, carried, out_near, out_far)
        if moment >= sections - 1:
            sent = [lax.ppermute(finished, "section", [(sections - 1, t)]) for t in (0, 2)]
            if moment == sections - 1:
                relayed = sent[0]
            else:
                sent.append(lax.ppermute(finished, "section", [(sections - 1, 1)]))
            memory += [finished] + sent
        if moment < MB + sections - 2:
            carried = lax.ppermute(finished, "section", onward)

    pieces = pl.pallas_call(
        cross_kernel,
        out_shape=shape((7 * tokens, 2 * HD)),
        in_specs=[SMEM] + [VMEM] * 10,
        out_specs=VMEM,
        compiler_params=PARAMS,
        name="cross",
    )(place, queries, w_cross, *memory)
    everyone = lax.all_gather(pieces, "tm", axis=0)
    context, grad = pl.pallas_call(
        combine_kernel,
        out_shape=(
            shape((MB * tokens, head_width)),
            shape((groups, 16, padded)),
        ),
        in_specs=[SMEM, SMEM, VMEM, VMEM],
        out_specs=(VMEM, VMEM),
        scratch_shapes=[pltpu.VMEM((shards * MB, tokens, 2 * HD), F32)] * 3
        + [pltpu.VMEM((shards, MB * tokens, padded), BF16)],
        compiler_params=PARAMS,
        name="combine",
    )(place, span_segment.reshape(-1), everyone, cot_cols)
    grad = lax.all_to_all(grad, "dp", 0, 0, tiled=True)
    grad_shard = jnp.sum(grad.astype(F32), axis=0)[:each, :head_width].T
    return (context, grad_shard)


def solution(mesh):
    in_specs = (
        P("dp", "tm", None),
        P("dp", "tm", None),
        P("dp", None),
        P(("dp", "tm"), None),
        P("section", ("dp", "tm"), None),
        P("section", None, ("dp", "tm")),
        P(("dp", "tm"), "section"),
        P(("dp", "tm"), "section"),
        P(("dp", "tm"), "section"),
        P(("dp", "tm"), None),
    )
    out_specs = (P(("dp", "tm"), "section"), P("section", ("dp", "tm")))
    return jax.shard_map(
        per_device, mesh=mesh, in_specs=in_specs, out_specs=out_specs, check_vma=False
    )
```

```python
import functools

import jax
import jax.numpy as jnp
from jax import lax
from jax.experimental import pallas as pl
from jax.experimental.pallas import tpu as pltpu
from jax.sharding import PartitionSpec as P

HD = 64
BLK = 64
MB = 2
EPS = 1e-05
F32 = jnp.float32
BF16 = jnp.bfloat16
VMEM = pl.BlockSpec(memory_space=pltpu.VMEM)
SMEM = pl.BlockSpec(memory_space=pltpu.SMEM)
PARAMS = pltpu.CompilerParams(vmem_limit_bytes=16 * 1024 * 1024)


def normed_rows(values):
    wide = values.astype(F32)
    center = wide - jnp.mean(wide, axis=-1, keepdims=True)
    spread = jnp.mean(center * center, axis=-1, keepdims=True)
    return (center * lax.rsqrt(spread + EPS)).astype(BF16)


def matmul(a, b):
    return jnp.dot(a, b, preferred_element_type=F32)


def matmul_nt(a, b):
    return lax.dot_general(a, b, (((1,), (1,)), ((), ())), preferred_element_type=F32)


def join_kernel(*refs):
    pieces, outs, sems = refs[:-4], refs[-4:-1], refs[-1]
    copies = []
    start = 0
    for index, out_ref in enumerate(outs):
        cols = slice(start, start + out_ref.shape[1])
        start += out_ref.shape[1]
        row = 0
        for slot, piece in enumerate(pieces):
            height = piece.shape[0]
            copies.append(
                pltpu.make_async_copy(
                    piece.at[:, cols],
                    out_ref.at[pl.ds(row, height), :],
                    sems.at[index, slot],
                )
            )
            row += height
    for copy in copies:
        copy.start()
    for copy in copies:
        copy.wait()


def halves_product(n, near_ref, far_ref):
    half = near_ref.shape[0]
    return matmul(n[:, :half], near_ref[...]) + matmul(n[:, half:], far_ref[...])


def kv_kernel(x_ref, near_ref, far_ref, n_ref, first_ref, last_ref):
    n = normed_rows(x_ref[...])
    n_ref[...] = n
    kv = halves_product(n, near_ref, far_ref).astype(BF16)
    first_ref[...] = kv[:BLK]
    last_ref[...] = kv[BLK:]


def allowed_of(moment, halo, place_ref, mask_ref):
    base = 4 * jnp.clip(moment - place_ref[0], 0, MB - 1)
    shard = place_ref[2]
    row = lax.broadcasted_iota(jnp.int32, (4 * BLK, 2 * BLK), 0)
    col = lax.broadcasted_iota(jnp.int32, (4 * BLK, 2 * BLK), 1)
    same = ((row // BLK) % 2 == 0) == (col < BLK)
    low_row = (row // BLK) % 2 == 0
    if halo:
        before = jnp.where(shard > 0, mask_ref[base], 0)
        after = jnp.where(shard < place_ref[5], mask_ref[base + 3], 0)
        open_side = jnp.where(low_row, before, after) == 1
        return same & open_side
    open_side = jnp.where(low_row, mask_ref[base + 1], mask_ref[base + 2]) == 1
    return same | open_side


def pair_attention(q, k, v, allowed):
    rows = q.shape[0]
    low = lax.broadcasted_iota(jnp.int32, q.shape, 1) < HD
    zero = jnp.zeros_like(q)
    both = jnp.concatenate([jnp.where(low, q, zero), jnp.where(low, zero, q)], axis=0)
    scores = matmul_nt(both, k) * HD ** (-0.5)
    weights = jnp.where(allowed, jnp.exp(scores), 0.0)
    totals = jnp.sum(weights, axis=-1, keepdims=True)
    summed = matmul(weights.astype(BF16), v)
    return (
        jnp.where(low, summed[:rows], summed[rows:]),
        jnp.where(low, totals[:rows], totals[rows:]),
    )


def own_kernel(
    moment, place_ref, mask_ref, n_ref, first_ref, last_ref, near_ref, far_ref, q_ref, num_ref, den_ref
):
    width = q_ref.shape[1]
    allowed = allowed_of(moment, False, place_ref, mask_ref)
    q = halves_product(n_ref[...], near_ref, far_ref).astype(BF16)
    q_ref[...] = q
    for lane in range(0, width, 2 * HD):
        cols = slice(lane, lane + 2 * HD)
        vcols = slice(width + lane, width + lane + 2 * HD)
        k = jnp.concatenate([first_ref[:, cols], last_ref[:, cols]], axis=0)
        v = jnp.concatenate([first_ref[:, vcols], last_ref[:, vcols]], axis=0)
        num_ref[:, cols], den_ref[:, cols] = pair_attention(q[:, cols], k, v, allowed)


def out_kernel(
    moment, place_ref, mask_ref, q_ref, num_ref, den_ref, left_ref, right_ref, x_ref, near_ref, far_ref,
    o_ref, ctx_ref
):
    width = q_ref.shape[1]
    allowed = allowed_of(moment, True, place_ref, mask_ref)
    for lane in range(0, width, 2 * HD):
        cols = slice(lane, lane + 2 * HD)
        vcols = slice(width + lane, width + lane + 2 * HD)
        k = jnp.concatenate([left_ref[:, cols], right_ref[:, cols]], axis=0)
        v = jnp.concatenate([left_ref[:, vcols], right_ref[:, vcols]], axis=0)
        num, den = pair_attention(q_ref[:, cols], k, v, allowed)
        ctx_ref[:, cols] = ((num + num_ref[:, cols]) / (den + den_ref[:, cols])).astype(BF16)
    half = near_ref.shape[0]
    for cols, w_ref in ((slice(0, half), near_ref), (slice(half, 2 * half), far_ref)):
        update = matmul_nt(ctx_ref[...], w_ref[...])
        o_ref[:, cols] = (x_ref[:, cols].astype(F32) + update).astype(BF16)


def order_kernel(order_ref, frames_ref, *out_refs):
    seqs, rows, model = frames_ref.shape
    frames = frames_ref[...].reshape(seqs * rows, model)
    for lane in range(0, model, 256):
        source = lax.broadcasted_iota(jnp.int32, (model, 256), 0)
        hit = source == order_ref[:, lane : lane + 256]
        pick = jnp.where(hit, 1.0, 0.0).astype(BF16)
        moved = matmul(frames, pick).astype(BF16)
        for seq, out_ref in enumerate(out_refs):
            out_ref[:, lane : lane + 256] = moved[seq * rows : (seq + 1) * rows]


def reorder_kernel(order_ref, w_ref, out_ref):
    model = w_ref.shape[0]
    for row in range(0, model, 256):
        source = lax.broadcasted_iota(jnp.int32, (256, model), 1)
        hit = source == order_ref[row : row + 256, :]
        pick = jnp.where(hit, 1.0, 0.0).astype(BF16)
        out_ref[row : row + 256, :] = matmul(pick, w_ref[...]).astype(BF16)


def query_kernel(seg_ref, dec_ref, w_ref, q_ref):
    q_ref[...] = matmul(normed_rows(dec_ref[...]), w_ref[...]).astype(BF16)


def cross_kernel(place_ref, q_ref, w_ref, *refs):
    parts, out_ref = refs[:-1], refs[-1]
    owner = place_ref[0] == place_ref[1]
    rows = []
    for start in (0, 4):
        own, a, b, c = (ref[...] for ref in parts[start : start + 4])
        rows.append(jnp.where(owner, own, a + b + c))
    n = normed_rows(jnp.concatenate(rows, axis=0))
    width = q_ref.shape[1]
    both = matmul(n, w_ref[...]).astype(BF16)
    keys, values = both[:, :width], both[:, width:]
    tokens = q_ref.shape[0] // 4
    heads = 3
    lane = lax.broadcasted_iota(jnp.int32, (tokens, width), 1)
    near = lax.broadcasted_iota(jnp.int32, (tokens, 2 * HD), 1)
    sums = jnp.zeros((tokens, 2 * HD), F32)
    thirds = []
    for piece in range(4):
        q = q_ref[piece * tokens : (piece + 1) * tokens, :]
        spots = slice(piece * BLK, (piece + 1) * BLK)
        stacked = jnp.concatenate(
            [jnp.where(lane // HD == head, q, jnp.zeros_like(q)) for head in range(heads)], axis=0
        )
        weights = jnp.exp(matmul_nt(stacked, keys[spots]) * HD ** (-0.5))
        totals = jnp.sum(weights, axis=-1, keepdims=True)
        summed = matmul(weights.astype(BF16), values[spots])
        high = totals.astype(BF16).astype(F32)
        rest = totals - high
        for head in range(heads):
            mine = slice(head * tokens, (head + 1) * tokens)
            sums = jnp.where(near == 32 * piece + head, high[mine], sums)
            sums = jnp.where(near == 32 * piece + heads + head, rest[mine], sums)
        pair = jnp.where(near < HD, summed[:tokens, : 2 * HD], summed[tokens : 2 * tokens, : 2 * HD])
        out_ref[piece * tokens : (piece + 1) * tokens, :] = pair.astype(BF16)
        thirds.append(summed[2 * tokens :, 2 * HD :])
    at = 4 * tokens
    for block in range(2):
        shifted = pltpu.roll(thirds[2 + block], HD, 1)
        out_ref[at + block * tokens : at + (block + 1) * tokens, :] = jnp.where(
            near < HD, thirds[block], shifted
        ).astype(BF16)
    out_ref[at + 2 * tokens :, :] = sums.astype(BF16)


def combine_kernel(
    place_ref, span_ref, parts_ref, cot_ref, ctx_ref, grad_ref, pair_ref, third_ref, sum_ref, all_ref
):
    shards = parts_ref.shape[0]
    tokens = pair_ref.shape[1]
    heads = 3
    for ref in (pair_ref, third_ref, sum_ref):
        ref[...] = jnp.zeros_like(ref)
    lane = lax.broadcasted_iota(jnp.int32, (tokens, 2 * HD), 1)
    for shard in range(shards):
        sums = parts_ref[shard, 6 * tokens : 7 * tokens, :].astype(F32)
        for seq in range(MB):
            for block in range(2):
                segment = span_ref[seq * 2 * shards + shard * 2 + block]
                spot = segment * MB + seq
                piece = seq * 2 + block
                pair = parts_ref[shard, piece * tokens : (piece + 1) * tokens, :]
                third = parts_ref[shard, (4 + block) * tokens : (5 + block) * tokens, :]
                pair_ref[spot] = pair_ref[spot] + pair.astype(F32)
                third_ref[spot] = third_ref[spot] + third.astype(F32)
                sum_ref[spot] = sum_ref[spot] + jnp.where(lane // 32 == piece, sums, 0.0)
    count = shards * tokens
    near = lax.broadcasted_iota(jnp.int32, (count, 2 * HD), 1)
    for seq in range(MB):

        def taken(ref):
            return ref[...].reshape(shards, MB, tokens, 2 * HD)[:, seq].reshape(count, 2 * HD)

        sums = taken(sum_ref)

        def total(head):
            at = 64 * seq + head
            spots = (at, at + heads, at + 32, at + 32 + heads)
            return sum(sums[:, spot : spot + 1] for spot in spots)

        pair = taken(pair_ref) / jnp.where(near < HD, total(0), total(1))
        third = taken(third_ref) / total(2)
        if seq:
            third = pltpu.roll(third, HD, 1)
        third = jnp.where(near < HD, third, 0.0)
        rows = slice(seq * tokens, (seq + 1) * tokens)
        all_ref[:, rows, : 2 * HD] = pair.astype(BF16).reshape(shards, tokens, 2 * HD)
        all_ref[:, rows, 2 * HD :] = third.astype(BF16).reshape(shards, tokens, 2 * HD)
    ctx_ref[...] = all_ref[place_ref[2]][:, : heads * HD]
    context = all_ref[...].reshape(shards * MB * tokens, 4 * HD)
    grad = lax.dot_general(
        cot_ref[...], context, (((0,), (0,)), ((), ())), preferred_element_type=F32
    )
    grad_ref[...] = grad.reshape(grad_ref.shape).astype(BF16)


def columns_kernel(place_ref, cot_ref, out_ref):
    cols = cot_ref.shape[1]
    lanes = out_ref.shape[1]
    each = place_ref[3]
    row = lax.broadcasted_iota(jnp.int32, (cols, lanes), 0)
    lane = lax.broadcasted_iota(jnp.int32, (cols, lanes), 1)
    inside = lane % 16
    hit = (row == (lane // 16) * place_ref[4] + place_ref[2] * each + inside) & (inside < each)
    out_ref[...] = matmul(cot_ref[...], jnp.where(hit, 1.0, 0.0).astype(BF16)).astype(BF16)


def shape(dims, dtype=BF16):
    return jax.ShapeDtypeStruct(dims, dtype)


def per_device(
    frames,
    block_mask,
    span_segment,
    dec_states,
    enc_qkv,
    enc_out,
    cross_query,
    cross_key,
    cross_value,
    cotangent,
):
    sections = lax.axis_size("section")
    shards = lax.axis_size("tm")
    groups = lax.axis_size("dp")
    section = lax.axis_index("section")
    shard = lax.axis_index("tm")
    model = frames.shape[2]
    width = enc_out.shape[1]
    head_width = cross_query.shape[1]
    padded = 256

    def pad_lanes(w):
        return jnp.pad(w, ((0, 0), (0, padded - w.shape[1])))

    def around(value, axis, size, step):
        return lax.ppermute(value, axis, [(i, (i + step) % size) for i in range(size)])

    own = jnp.concatenate([enc_qkv[0], enc_out[0].T], axis=1)
    lanes = own.reshape(-1, 128)
    block = lax.all_to_all(
        jnp.broadcast_to(lanes[None], (groups,) + lanes.shape), "dp", 0, 0, tiled=True
    ).reshape(groups * own.shape[0], own.shape[1])
    chips = shards // 2
    ring, source = [block], [shard]
    ends = []
    for step in (2, -2):
        moving = block
        for hop in range(chips // 2 - 1):
            moving = around(moving, "tm", shards, step)
            ring.append(moving)
            source.append((shard - step * (hop + 1)) % shards)
        ends.append(moving)
    cut = block.shape[0] * 3 // 5
    ring.append(around(ends[0][:cut], "tm", shards, 2))
    ring.append(around(ends[1][cut:], "tm", shards, -2))
    source.append((shard + chips) % shards)
    source = jnp.stack(source + [place ^ 1 for place in source])
    each = model // (groups * shards)
    slots = jnp.arange(groups)
    order = (slots[None, :, None] * shards + source[:, None, None]) * each + jnp.arange(each)
    order = order.reshape(-1).astype(jnp.int32)

    half = model // 2
    q_near, kv_near, out_near = pl.pallas_call(
        join_kernel,
        out_shape=(shape((half, width)), shape((half, 2 * width)), shape((half, width))),
        in_specs=[pl.BlockSpec(memory_space=pl.ANY)] * len(ring),
        out_specs=(VMEM,) * 3,
        scratch_shapes=[pltpu.SemaphoreType.DMA((3, len(ring)))],
        compiler_params=pltpu.CompilerParams(),
        name="join",
    )(*ring)
    swap = [(i, i ^ 1) for i in range(shards)]
    kv_far, q_far, out_far = (lax.ppermute(w, "tm", swap) for w in (kv_near, q_near, out_near))

    cross = jnp.concatenate([pad_lanes(w) for w in (cross_key, cross_value, cross_query)], axis=1)
    cross = lax.all_gather(cross, ("dp", "tm"), axis=0, tiled=True)
    tokens_all = lax.all_gather(
        jnp.concatenate([dec_states, cotangent], axis=1), "tm", axis=0, tiled=True
    )

    place = jnp.stack(
        [
            section,
            jnp.int32(sections - 1),
            shard,
            jnp.int32(each),
            jnp.int32(each * shards),
            jnp.int32(shards - 1),
        ]
    ).astype(jnp.int32)
    mask = block_mask.reshape(-1)
    inputs = pl.pallas_call(
        order_kernel,
        out_shape=(shape(frames.shape[1:]),) * MB,
        in_specs=[VMEM, VMEM],
        out_specs=(VMEM,) * MB,
        compiler_params=PARAMS,
        name="order",
    )(order.reshape(1, -1), frames)

    up = [(i, i + 1) for i in range(shards - 1)]
    down = [(i + 1, i) for i in range(shards - 1)]
    onward = [(i, i + 1) for i in range(sections - 1)]
    rows = frames.shape[1]
    tokens = dec_states.shape[0] // MB
    carried = inputs[0]
    memory = []
    for moment in range(MB + sections - 1):
        if moment == 1:
            carried, cross = lax.optimization_barrier((carried, cross))
        if 0 < moment < MB:
            carried = jnp.where(section == 0, inputs[moment], carried)
        if moment == 2:
            w_cross = pl.pallas_call(
                reorder_kernel,
                grid=(1,),
                out_shape=shape((model, 2 * padded)),
                in_specs=[
                    pl.BlockSpec((model, 1), lambda i: (0, 0)),
                    pl.BlockSpec((model, 2 * padded), lambda i: (0, 0)),
                ],
                out_specs=pl.BlockSpec((model, 2 * padded), lambda i: (0, 0)),
                compiler_params=PARAMS,
                name="reorder",
            )(order.reshape(-1, 1), cross)
            carried, w_cross = lax.optimization_barrier((carried, w_cross))
        if moment == 3:
            mine = lax.dynamic_slice_in_dim(span_segment, shard * 2, 2, axis=1).reshape(-1)
            queries = pl.pallas_call(
                query_kernel,
                grid_spec=pltpu.PrefetchScalarGridSpec(
                    num_scalar_prefetch=1,
                    grid=(4,),
                    in_specs=[
                        pl.BlockSpec((tokens, model), lambda i, seg: (seg[i] * MB + i // 2, 0)),
                        pl.BlockSpec((model, padded), lambda i, seg: (0, 2)),
                    ],
                    out_specs=pl.BlockSpec((tokens, padded), lambda i, seg: (i, 0)),
                ),
                out_shape=shape((4 * tokens, padded)),
                compiler_params=PARAMS,
                name="queries",
            )(mine, tokens_all, cross)
            carried, queries = lax.optimization_barrier((carried, queries))
        if moment == 4:
            cot_cols = pl.pallas_call(
                columns_kernel,
                grid=(1,),
                out_shape=shape((shards * MB * tokens, groups * 16)),
                in_specs=[
                    SMEM,
                    pl.BlockSpec((shards * MB * tokens, model), lambda i: (0, 1)),
                ],
                out_specs=pl.BlockSpec((shards * MB * tokens, groups * 16), lambda i: (0, 0)),
                compiler_params=PARAMS,
                name="columns",
            )(place, tokens_all)
            carried, cot_cols = lax.optimization_barrier((carried, cot_cols))

        n, first, last = pl.pallas_call(
            kv_kernel,
            out_shape=(shape((rows, model)), shape((BLK, 2 * width)), shape((BLK, 2 * width))),
            in_specs=[VMEM] * 3,
            out_specs=(VMEM, VMEM, VMEM),
            compiler_params=PARAMS,
            name="keys_values",
        )(carried, kv_near, kv_far)
        left = lax.ppermute(last, "tm", up)
        right = lax.ppermute(first, "tm", down)
        q, num, den = pl.pallas_call(
            functools.partial(own_kernel, moment),
            out_shape=(shape((rows, width)), shape((rows, width), F32), shape((rows, width), F32)),
            in_specs=[SMEM, SMEM] + [VMEM] * 5,
            out_specs=(VMEM, VMEM, VMEM),
            compiler_params=PARAMS,
            name="own_blocks",
        )(place, mask, n, first, last, q_near, q_far)
        if moment == sections:
            q, relayed = lax.optimization_barrier((q, relayed))
            memory.append(lax.ppermute(relayed, "section", [(0, 1)]))
        finished = pl.pallas_call(
            functools.partial(out_kernel, moment),
            out_shape=shape((rows, model)),
            in_specs=[SMEM, SMEM] + [VMEM] * 8,
            out_specs=VMEM,
            scratch_shapes=[pltpu.VMEM((rows, width), BF16)],
            compiler_params=PARAMS,
            name="layer_out",
        )(place, mask, q, num, den, left, right, carried, out_near, out_far)
        if moment >= sections - 1:
            sent = [lax.ppermute(finished, "section", [(sections - 1, t)]) for t in (0, 2)]
            if moment == sections - 1:
                relayed = sent[0]
            else:
                sent.append(lax.ppermute(finished, "section", [(sections - 1, 1)]))
            memory += [finished] + sent
        if moment < MB + sections - 2:
            carried = lax.ppermute(finished, "section", onward)

    pieces = pl.pallas_call(
        cross_kernel,
        out_shape=shape((7 * tokens, 2 * HD)),
        in_specs=[SMEM] + [VMEM] * 10,
        out_specs=VMEM,
        compiler_params=PARAMS,
        name="cross",
    )(place, queries, w_cross, *memory)
    everyone = lax.all_gather(pieces, "tm", axis=0)
    context, grad = pl.pallas_call(
        combine_kernel,
        out_shape=(
            shape((MB * tokens, head_width)),
            shape((groups, 16, padded)),
        ),
        in_specs=[SMEM, SMEM, VMEM, VMEM],
        out_specs=(VMEM, VMEM),
        scratch_shapes=[pltpu.VMEM((shards * MB, tokens, 2 * HD), F32)] * 3
        + [pltpu.VMEM((shards, MB * tokens, padded), BF16)],
        compiler_params=PARAMS,
        name="combine",
    )(place, span_segment.reshape(-1), everyone, cot_cols)
    grad = lax.all_to_all(grad, "dp", 0, 0, tiled=True)
    grad_shard = jnp.sum(grad.astype(F32), axis=0)[:each, :head_width].T
    return (context, grad_shard)


def solution(mesh):
    in_specs = (
        P("dp", "tm", None),
        P("dp", "tm", None),
        P("dp", None),
        P(("dp", "tm"), None),
        P("section", ("dp", "tm"), None),
        P("section", None, ("dp", "tm")),
        P(("dp", "tm"), "section"),
        P(("dp", "tm"), "section"),
        P(("dp", "tm"), "section"),
        P(("dp", "tm"), None),
    )
    out_specs = (P(("dp", "tm"), "section"), P("section", ("dp", "tm")))
    return jax.shard_map(
        per_device, mesh=mesh, in_specs=in_specs, out_specs=out_specs, check_vma=False
    )
```

```python
import functools

import jax
import jax.numpy as jnp
from jax import lax
from jax.experimental import pallas as pl
from jax.experimental.pallas import tpu as pltpu
from jax.sharding import PartitionSpec as P

HD = 64
BLK = 64
MB = 2
EPS = 1e-05
F32 = jnp.float32
BF16 = jnp.bfloat16
VMEM = pl.BlockSpec(memory_space=pltpu.VMEM)
SMEM = pl.BlockSpec(memory_space=pltpu.SMEM)
PARAMS = pltpu.CompilerParams(vmem_limit_bytes=16 * 1024 * 1024)


def normed_rows(values):
    wide = values.astype(F32)
    center = wide - jnp.mean(wide, axis=-1, keepdims=True)
    spread = jnp.mean(center * center, axis=-1, keepdims=True)
    return (center * lax.rsqrt(spread + EPS)).astype(BF16)


def matmul(a, b):
    return jnp.dot(a, b, preferred_element_type=F32)


def matmul_nt(a, b):
    return lax.dot_general(a, b, (((1,), (1,)), ((), ())), preferred_element_type=F32)


def join_kernel(*refs):
    pieces, outs, sems = refs[:-4], refs[-4:-1], refs[-1]
    copies = []
    start = 0
    for index, out_ref in enumerate(outs):
        cols = slice(start, start + out_ref.shape[1])
        start += out_ref.shape[1]
        row = 0
        for slot, piece in enumerate(pieces):
            height = piece.shape[0]
            copies.append(
                pltpu.make_async_copy(
                    piece.at[:, cols],
                    out_ref.at[pl.ds(row, height), :],
                    sems.at[index, slot],
                )
            )
            row += height
    for copy in copies:
        copy.start()
    for copy in copies:
        copy.wait()


def halves_product(n, near_ref, far_ref):
    half = near_ref.shape[0]
    return matmul(n[:, :half], near_ref[...]) + matmul(n[:, half:], far_ref[...])


def kv_kernel(x_ref, near_ref, far_ref, n_ref, first_ref, last_ref):
    n = normed_rows(x_ref[...])
    n_ref[...] = n
    kv = halves_product(n, near_ref, far_ref).astype(BF16)
    first_ref[...] = kv[:BLK]
    last_ref[...] = kv[BLK:]


def allowed_of(moment, halo, place_ref, mask_ref):
    base = 4 * jnp.clip(moment - place_ref[0], 0, MB - 1)
    shard = place_ref[2]
    row = lax.broadcasted_iota(jnp.int32, (4 * BLK, 2 * BLK), 0)
    col = lax.broadcasted_iota(jnp.int32, (4 * BLK, 2 * BLK), 1)
    same = ((row // BLK) % 2 == 0) == (col < BLK)
    low_row = (row // BLK) % 2 == 0
    if halo:
        before = jnp.where(shard > 0, mask_ref[base], 0)
        after = jnp.where(shard < place_ref[5], mask_ref[base + 3], 0)
        open_side = jnp.where(low_row, before, after) == 1
        return same & open_side
    open_side = jnp.where(low_row, mask_ref[base + 1], mask_ref[base + 2]) == 1
    return same | open_side


def pair_attention(q, k, v, allowed):
    rows = q.shape[0]
    low = lax.broadcasted_iota(jnp.int32, q.shape, 1) < HD
    zero = jnp.zeros_like(q)
    both = jnp.concatenate([jnp.where(low, q, zero), jnp.where(low, zero, q)], axis=0)
    scores = matmul_nt(both, k) * HD ** (-0.5)
    weights = jnp.where(allowed, jnp.exp(scores), 0.0)
    totals = jnp.sum(weights, axis=-1, keepdims=True)
    summed = matmul(weights.astype(BF16), v)
    return (
        jnp.where(low, summed[:rows], summed[rows:]),
        jnp.where(low, totals[:rows], totals[rows:]),
    )


def own_kernel(
    moment, place_ref, mask_ref, n_ref, first_ref, last_ref, near_ref, far_ref, q_ref, num_ref, den_ref
):
    width = q_ref.shape[1]
    allowed = allowed_of(moment, False, place_ref, mask_ref)
    q = halves_product(n_ref[...], near_ref, far_ref).astype(BF16)
    q_ref[...] = q
    for lane in range(0, width, 2 * HD):
        cols = slice(lane, lane + 2 * HD)
        vcols = slice(width + lane, width + lane + 2 * HD)
        k = jnp.concatenate([first_ref[:, cols], last_ref[:, cols]], axis=0)
        v = jnp.concatenate([first_ref[:, vcols], last_ref[:, vcols]], axis=0)
        num_ref[:, cols], den_ref[:, cols] = pair_attention(q[:, cols], k, v, allowed)


def out_kernel(
    moment, place_ref, mask_ref, q_ref, num_ref, den_ref, left_ref, right_ref, x_ref, near_ref, far_ref,
    o_ref, ctx_ref
):
    width = q_ref.shape[1]
    allowed = allowed_of(moment, True, place_ref, mask_ref)
    for lane in range(0, width, 2 * HD):
        cols = slice(lane, lane + 2 * HD)
        vcols = slice(width + lane, width + lane + 2 * HD)
        k = jnp.concatenate([left_ref[:, cols], right_ref[:, cols]], axis=0)
        v = jnp.concatenate([left_ref[:, vcols], right_ref[:, vcols]], axis=0)
        num, den = pair_attention(q_ref[:, cols], k, v, allowed)
        ctx_ref[:, cols] = ((num + num_ref[:, cols]) / (den + den_ref[:, cols])).astype(BF16)
    half = near_ref.shape[0]
    for cols, w_ref in ((slice(0, half), near_ref), (slice(half, 2 * half), far_ref)):
        update = matmul_nt(ctx_ref[...], w_ref[...])
        o_ref[:, cols] = (x_ref[:, cols].astype(F32) + update).astype(BF16)


def order_kernel(order_ref, frames_ref, *out_refs):
    seqs, rows, model = frames_ref.shape
    frames = frames_ref[...].reshape(seqs * rows, model)
    for lane in range(0, model, 256):
        source = lax.broadcasted_iota(jnp.int32, (model, 256), 0)
        hit = source == order_ref[:, lane : lane + 256]
        pick = jnp.where(hit, 1.0, 0.0).astype(BF16)
        moved = matmul(frames, pick).astype(BF16)
        for seq, out_ref in enumerate(out_refs):
            out_ref[:, lane : lane + 256] = moved[seq * rows : (seq + 1) * rows]


def reorder_kernel(order_ref, w_ref, out_ref):
    model = w_ref.shape[0]
    for row in range(0, model, 256):
        source = lax.broadcasted_iota(jnp.int32, (256, model), 1)
        hit = source == order_ref[row : row + 256, :]
        pick = jnp.where(hit, 1.0, 0.0).astype(BF16)
        out_ref[row : row + 256, :] = matmul(pick, w_ref[...]).astype(BF16)


def query_kernel(seg_ref, dec_ref, w_ref, q_ref):
    q_ref[...] = matmul(normed_rows(dec_ref[...]), w_ref[...]).astype(BF16)


def cross_kernel(place_ref, q_ref, w_ref, *refs):
    parts, out_ref = refs[:-1], refs[-1]
    owner = place_ref[0] == place_ref[1]
    rows = []
    for start in (0, 4):
        own, a, b, c = (ref[...] for ref in parts[start : start + 4])
        rows.append(jnp.where(owner, own, a + b + c))
    n = normed_rows(jnp.concatenate(rows, axis=0))
    width = q_ref.shape[1]
    both = matmul(n, w_ref[...]).astype(BF16)
    keys, values = both[:, :width], both[:, width:]
    tokens = q_ref.shape[0] // 4
    heads = 3
    lane = lax.broadcasted_iota(jnp.int32, (tokens, width), 1)
    near = lax.broadcasted_iota(jnp.int32, (tokens, 2 * HD), 1)
    sums = jnp.zeros((tokens, 2 * HD), F32)
    thirds = []
    for piece in range(4):
        q = q_ref[piece * tokens : (piece + 1) * tokens, :]
        spots = slice(piece * BLK, (piece + 1) * BLK)
        stacked = jnp.concatenate(
            [jnp.where(lane // HD == head, q, jnp.zeros_like(q)) for head in range(heads)], axis=0
        )
        weights = jnp.exp(matmul_nt(stacked, keys[spots]) * HD ** (-0.5))
        totals = jnp.sum(weights, axis=-1, keepdims=True)
        summed = matmul(weights.astype(BF16), values[spots])
        high = totals.astype(BF16).astype(F32)
        rest = totals - high
        for head in range(heads):
            mine = slice(head * tokens, (head + 1) * tokens)
            sums = jnp.where(near == 32 * piece + head, high[mine], sums)
            sums = jnp.where(near == 32 * piece + heads + head, rest[mine], sums)
        pair = jnp.where(near < HD, summed[:tokens, : 2 * HD], summed[tokens : 2 * tokens, : 2 * HD])
        out_ref[piece * tokens : (piece + 1) * tokens, :] = pair.astype(BF16)
        thirds.append(summed[2 * tokens :, 2 * HD :])
    at = 4 * tokens
    for block in range(2):
        shifted = pltpu.roll(thirds[2 + block], HD, 1)
        out_ref[at + block * tokens : at + (block + 1) * tokens, :] = jnp.where(
            near < HD, thirds[block], shifted
        ).astype(BF16)
    out_ref[at + 2 * tokens :, :] = sums.astype(BF16)


def combine_kernel(
    place_ref, span_ref, parts_ref, cot_ref, ctx_ref, grad_ref, pair_ref, third_ref, sum_ref, all_ref
):
    shards = parts_ref.shape[0]
    tokens = pair_ref.shape[1]
    heads = 3
    for ref in (pair_ref, third_ref, sum_ref):
        ref[...] = jnp.zeros_like(ref)
    lane = lax.broadcasted_iota(jnp.int32, (tokens, 2 * HD), 1)
    for shard in range(shards):
        sums = parts_ref[shard, 6 * tokens : 7 * tokens, :].astype(F32)
        for seq in range(MB):
            for block in range(2):
                segment = span_ref[seq * 2 * shards + shard * 2 + block]
                spot = segment * MB + seq
                piece = seq * 2 + block
                pair = parts_ref[shard, piece * tokens : (piece + 1) * tokens, :]
                third = parts_ref[shard, (4 + block) * tokens : (5 + block) * tokens, :]
                pair_ref[spot] = pair_ref[spot] + pair.astype(F32)
                third_ref[spot] = third_ref[spot] + third.astype(F32)
                sum_ref[spot] = sum_ref[spot] + jnp.where(lane // 32 == piece, sums, 0.0)
    count = shards * tokens
    near = lax.broadcasted_iota(jnp.int32, (count, 2 * HD), 1)
    for seq in range(MB):

        def taken(ref):
            return ref[...].reshape(shards, MB, tokens, 2 * HD)[:, seq].reshape(count, 2 * HD)

        sums = taken(sum_ref)

        def total(head):
            at = 64 * seq + head
            spots = (at, at + heads, at + 32, at + 32 + heads)
            return sum(sums[:, spot : spot + 1] for spot in spots)

        pair = taken(pair_ref) / jnp.where(near < HD, total(0), total(1))
        third = taken(third_ref) / total(2)
        if seq:
            third = pltpu.roll(third, HD, 1)
        third = jnp.where(near < HD, third, 0.0)
        rows = slice(seq * tokens, (seq + 1) * tokens)
        all_ref[:, rows, : 2 * HD] = pair.astype(BF16).reshape(shards, tokens, 2 * HD)
        all_ref[:, rows, 2 * HD :] = third.astype(BF16).reshape(shards, tokens, 2 * HD)
    ctx_ref[...] = all_ref[place_ref[2]][:, : heads * HD]
    context = all_ref[...].reshape(shards * MB * tokens, 4 * HD)
    grad = lax.dot_general(
        cot_ref[...], context, (((0,), (0,)), ((), ())), preferred_element_type=F32
    )
    grad_ref[...] = grad.reshape(grad_ref.shape).astype(BF16)


def columns_kernel(place_ref, cot_ref, out_ref):
    cols = cot_ref.shape[1]
    lanes = out_ref.shape[1]
    each = place_ref[3]
    row = lax.broadcasted_iota(jnp.int32, (cols, lanes), 0)
    lane = lax.broadcasted_iota(jnp.int32, (cols, lanes), 1)
    inside = lane % 16
    hit = (row == (lane // 16) * place_ref[4] + place_ref[2] * each + inside) & (inside < each)
    out_ref[...] = matmul(cot_ref[...], jnp.where(hit, 1.0, 0.0).astype(BF16)).astype(BF16)


def shape(dims, dtype=BF16):
    return jax.ShapeDtypeStruct(dims, dtype)


def per_device(
    frames,
    block_mask,
    span_segment,
    dec_states,
    enc_qkv,
    enc_out,
    cross_query,
    cross_key,
    cross_value,
    cotangent,
):
    sections = lax.axis_size("section")
    shards = lax.axis_size("tm")
    groups = lax.axis_size("dp")
    section = lax.axis_index("section")
    shard = lax.axis_index("tm")
    model = frames.shape[2]
    width = enc_out.shape[1]
    head_width = cross_query.shape[1]
    padded = 256

    def pad_lanes(w):
        return jnp.pad(w, ((0, 0), (0, padded - w.shape[1])))

    def around(value, axis, size, step):
        return lax.ppermute(value, axis, [(i, (i + step) % size) for i in range(size)])

    own = jnp.concatenate([enc_qkv[0], enc_out[0].T], axis=1)
    lanes = own.reshape(-1, 128)
    block = lax.all_to_all(
        jnp.broadcast_to(lanes[None], (groups,) + lanes.shape), "dp", 0, 0, tiled=True
    ).reshape(groups * own.shape[0], own.shape[1])
    chips = shards // 2
    ring, source = [block], [shard]
    ends = []
    for step in (2, -2):
        moving = block
        for hop in range(chips // 2 - 1):
            moving = around(moving, "tm", shards, step)
            ring.append(moving)
            source.append((shard - step * (hop + 1)) % shards)
        ends.append(moving)
    cut = block.shape[0] * 3 // 5
    ring.append(around(ends[0][:cut], "tm", shards, 2))
    ring.append(around(ends[1][cut:], "tm", shards, -2))
    source.append((shard + chips) % shards)
    source = jnp.stack(source + [place ^ 1 for place in source])
    each = model // (groups * shards)
    slots = jnp.arange(groups)
    order = (slots[None, :, None] * shards + source[:, None, None]) * each + jnp.arange(each)
    order = order.reshape(-1).astype(jnp.int32)

    inputs = pl.pallas_call(
        order_kernel,
        out_shape=(shape(frames.shape[1:]),) * MB,
        in_specs=[VMEM, VMEM],
        out_specs=(VMEM,) * MB,
        compiler_params=PARAMS,
        name="order",
    )(order.reshape(1, -1), frames)

    ring[-1], *inputs = lax.optimization_barrier((ring[-1], *inputs))
    half = model // 2
    q_near, kv_near, out_near = pl.pallas_call(
        join_kernel,
        out_shape=(shape((half, width)), shape((half, 2 * width)), shape((half, width))),
        in_specs=[pl.BlockSpec(memory_space=pl.ANY)] * len(ring),
        out_specs=(VMEM,) * 3,
        scratch_shapes=[pltpu.SemaphoreType.DMA((3, len(ring)))],
        compiler_params=pltpu.CompilerParams(),
        name="join",
    )(*ring)
    swap = [(i, i ^ 1) for i in range(shards)]
    kv_far, q_far, out_far = (lax.ppermute(w, "tm", swap) for w in (kv_near, q_near, out_near))

    cross = jnp.concatenate([pad_lanes(w) for w in (cross_key, cross_value, cross_query)], axis=1)
    cross = lax.all_gather(cross, ("dp", "tm"), axis=0, tiled=True)
    tokens_all = lax.all_gather(
        jnp.concatenate([dec_states, cotangent], axis=1), "tm", axis=0, tiled=True
    )

    place = jnp.stack(
        [
            section,
            jnp.int32(sections - 1),
            shard,
            jnp.int32(each),
            jnp.int32(each * shards),
            jnp.int32(shards - 1),
        ]
    ).astype(jnp.int32)
    mask = block_mask.reshape(-1)
    up = [(i, i + 1) for i in range(shards - 1)]
    down = [(i + 1, i) for i in range(shards - 1)]
    onward = [(i, i + 1) for i in range(sections - 1)]
    rows = frames.shape[1]
    tokens = dec_states.shape[0] // MB
    carried = inputs[0]
    memory = []
    for moment in range(MB + sections - 1):
        if moment == 1:
            carried, cross = lax.optimization_barrier((carried, cross))
        if 0 < moment < MB:
            carried = jnp.where(section == 0, inputs[moment], carried)
        if moment == 2:
            w_cross = pl.pallas_call(
                reorder_kernel,
                grid=(1,),
                out_shape=shape((model, 2 * padded)),
                in_specs=[
                    pl.BlockSpec((model, 1), lambda i: (0, 0)),
                    pl.BlockSpec((model, 2 * padded), lambda i: (0, 0)),
                ],
                out_specs=pl.BlockSpec((model, 2 * padded), lambda i: (0, 0)),
                compiler_params=PARAMS,
                name="reorder",
            )(order.reshape(-1, 1), cross)
            carried, w_cross = lax.optimization_barrier((carried, w_cross))
        if moment == 3:
            mine = lax.dynamic_slice_in_dim(span_segment, shard * 2, 2, axis=1).reshape(-1)
            queries = pl.pallas_call(
                query_kernel,
                grid_spec=pltpu.PrefetchScalarGridSpec(
                    num_scalar_prefetch=1,
                    grid=(4,),
                    in_specs=[
                        pl.BlockSpec((tokens, model), lambda i, seg: (seg[i] * MB + i // 2, 0)),
                        pl.BlockSpec((model, padded), lambda i, seg: (0, 2)),
                    ],
                    out_specs=pl.BlockSpec((tokens, padded), lambda i, seg: (i, 0)),
                ),
                out_shape=shape((4 * tokens, padded)),
                compiler_params=PARAMS,
                name="queries",
            )(mine, tokens_all, cross)
            carried, queries = lax.optimization_barrier((carried, queries))
        if moment == 4:
            cot_cols = pl.pallas_call(
                columns_kernel,
                grid=(1,),
                out_shape=shape((shards * MB * tokens, groups * 16)),
                in_specs=[
                    SMEM,
                    pl.BlockSpec((shards * MB * tokens, model), lambda i: (0, 1)),
                ],
                out_specs=pl.BlockSpec((shards * MB * tokens, groups * 16), lambda i: (0, 0)),
                compiler_params=PARAMS,
                name="columns",
            )(place, tokens_all)
            carried, cot_cols = lax.optimization_barrier((carried, cot_cols))

        n, first, last = pl.pallas_call(
            kv_kernel,
            out_shape=(shape((rows, model)), shape((BLK, 2 * width)), shape((BLK, 2 * width))),
            in_specs=[VMEM] * 3,
            out_specs=(VMEM, VMEM, VMEM),
            compiler_params=PARAMS,
            name="keys_values",
        )(carried, kv_near, kv_far)
        left = lax.ppermute(last, "tm", up)
        right = lax.ppermute(first, "tm", down)
        q, num, den = pl.pallas_call(
            functools.partial(own_kernel, moment),
            out_shape=(shape((rows, width)), shape((rows, width), F32), shape((rows, width), F32)),
            in_specs=[SMEM, SMEM] + [VMEM] * 5,
            out_specs=(VMEM, VMEM, VMEM),
            compiler_params=PARAMS,
            name="own_blocks",
        )(place, mask, n, first, last, q_near, q_far)
        if moment == sections:
            q, relayed = lax.optimization_barrier((q, relayed))
            memory.append(lax.ppermute(relayed, "section", [(0, 1)]))
        finished = pl.pallas_call(
            functools.partial(out_kernel, moment),
            out_shape=shape((rows, model)),
            in_specs=[SMEM, SMEM] + [VMEM] * 8,
            out_specs=VMEM,
            scratch_shapes=[pltpu.VMEM((rows, width), BF16)],
            compiler_params=PARAMS,
            name="layer_out",
        )(place, mask, q, num, den, left, right, carried, out_near, out_far)
        if moment >= sections - 1:
            sent = [lax.ppermute(finished, "section", [(sections - 1, t)]) for t in (0, 2)]
            if moment == sections - 1:
                relayed = sent[0]
            else:
                sent.append(lax.ppermute(finished, "section", [(sections - 1, 1)]))
            memory += [finished] + sent
        if moment < MB + sections - 2:
            carried = lax.ppermute(finished, "section", onward)

    pieces = pl.pallas_call(
        cross_kernel,
        out_shape=shape((7 * tokens, 2 * HD)),
        in_specs=[SMEM] + [VMEM] * 10,
        out_specs=VMEM,
        compiler_params=PARAMS,
        name="cross",
    )(place, queries, w_cross, *memory)
    everyone = lax.all_gather(pieces, "tm", axis=0)
    context, grad = pl.pallas_call(
        combine_kernel,
        out_shape=(
            shape((MB * tokens, head_width)),
            shape((groups, 16, padded)),
        ),
        in_specs=[SMEM, SMEM, VMEM, VMEM],
        out_specs=(VMEM, VMEM),
        scratch_shapes=[pltpu.VMEM((shards * MB, tokens, 2 * HD), F32)] * 3
        + [pltpu.VMEM((shards, MB * tokens, padded), BF16)],
        compiler_params=PARAMS,
        name="combine",
    )(place, span_segment.reshape(-1), everyone, cot_cols)
    grad = lax.all_to_all(grad, "dp", 0, 0, tiled=True)
    grad_shard = jnp.sum(grad.astype(F32), axis=0)[:each, :head_width].T
    return (context, grad_shard)


def solution(mesh):
    in_specs = (
        P("dp", "tm", None),
        P("dp", "tm", None),
        P("dp", None),
        P(("dp", "tm"), None),
        P("section", ("dp", "tm"), None),
        P("section", None, ("dp", "tm")),
        P(("dp", "tm"), "section"),
        P(("dp", "tm"), "section"),
        P(("dp", "tm"), "section"),
        P(("dp", "tm"), None),
    )
    out_specs = (P(("dp", "tm"), "section"), P("section", ("dp", "tm")))
    return jax.shard_map(
        per_device, mesh=mesh, in_specs=in_specs, out_specs=out_specs, check_vma=False
    )
```

```python
import functools

import jax
import jax.numpy as jnp
from jax import lax
from jax.experimental import pallas as pl
from jax.experimental.pallas import tpu as pltpu
from jax.sharding import PartitionSpec as P

HD = 64
BLK = 64
MB = 2
EPS = 1e-05
F32 = jnp.float32
BF16 = jnp.bfloat16
VMEM = pl.BlockSpec(memory_space=pltpu.VMEM)
SMEM = pl.BlockSpec(memory_space=pltpu.SMEM)
PARAMS = pltpu.CompilerParams(vmem_limit_bytes=16 * 1024 * 1024)


def normed_rows(values):
    wide = values.astype(F32)
    center = wide - jnp.mean(wide, axis=-1, keepdims=True)
    spread = jnp.mean(center * center, axis=-1, keepdims=True)
    return (center * lax.rsqrt(spread + EPS)).astype(BF16)


def matmul(a, b):
    return jnp.dot(a, b, preferred_element_type=F32)


def matmul_nt(a, b):
    return lax.dot_general(a, b, (((1,), (1,)), ((), ())), preferred_element_type=F32)


def join_kernel(*refs):
    pieces, outs, sems = refs[:-4], refs[-4:-1], refs[-1]
    copies = []
    start = 0
    for index, out_ref in enumerate(outs):
        cols = slice(start, start + out_ref.shape[1])
        start += out_ref.shape[1]
        row = 0
        for slot, piece in enumerate(pieces):
            height = piece.shape[0]
            copies.append(
                pltpu.make_async_copy(
                    piece.at[:, cols],
                    out_ref.at[pl.ds(row, height), :],
                    sems.at[index, slot],
                )
            )
            row += height
    for copy in copies:
        copy.start()
    for copy in copies:
        copy.wait()


def halves_product(n, near_ref, far_ref):
    half = near_ref.shape[0]
    return matmul(n[:, :half], near_ref[...]) + matmul(n[:, half:], far_ref[...])


def kv_kernel(x_ref, near_ref, far_ref, n_ref, first_ref, last_ref):
    n = normed_rows(x_ref[...])
    n_ref[...] = n
    kv = halves_product(n, near_ref, far_ref).astype(BF16)
    first_ref[...] = kv[:BLK]
    last_ref[...] = kv[BLK:]


def allowed_of(moment, halo, place_ref, mask_ref):
    base = 4 * jnp.clip(moment - place_ref[0], 0, MB - 1)
    shard = place_ref[2]
    row = lax.broadcasted_iota(jnp.int32, (4 * BLK, 2 * BLK), 0)
    col = lax.broadcasted_iota(jnp.int32, (4 * BLK, 2 * BLK), 1)
    same = ((row // BLK) % 2 == 0) == (col < BLK)
    low_row = (row // BLK) % 2 == 0
    if halo:
        before = jnp.where(shard > 0, mask_ref[base], 0)
        after = jnp.where(shard < place_ref[5], mask_ref[base + 3], 0)
        open_side = jnp.where(low_row, before, after) == 1
        return same & open_side
    open_side = jnp.where(low_row, mask_ref[base + 1], mask_ref[base + 2]) == 1
    return same | open_side


def pair_attention(q, k, v, allowed):
    rows = q.shape[0]
    low = lax.broadcasted_iota(jnp.int32, q.shape, 1) < HD
    zero = jnp.zeros_like(q)
    both = jnp.concatenate([jnp.where(low, q, zero), jnp.where(low, zero, q)], axis=0)
    scores = matmul_nt(both, k) * HD ** (-0.5)
    weights = jnp.where(allowed, jnp.exp(scores), 0.0)
    totals = jnp.sum(weights, axis=-1, keepdims=True)
    summed = matmul(weights.astype(BF16), v)
    return (
        jnp.where(low, summed[:rows], summed[rows:]),
        jnp.where(low, totals[:rows], totals[rows:]),
    )


def own_kernel(
    moment, place_ref, mask_ref, n_ref, first_ref, last_ref, near_ref, far_ref, q_ref, num_ref, den_ref
):
    width = q_ref.shape[1]
    allowed = allowed_of(moment, False, place_ref, mask_ref)
    q = halves_product(n_ref[...], near_ref, far_ref).astype(BF16)
    q_ref[...] = q
    for lane in range(0, width, 2 * HD):
        cols = slice(lane, lane + 2 * HD)
        vcols = slice(width + lane, width + lane + 2 * HD)
        k = jnp.concatenate([first_ref[:, cols], last_ref[:, cols]], axis=0)
        v = jnp.concatenate([first_ref[:, vcols], last_ref[:, vcols]], axis=0)
        num_ref[:, cols], den_ref[:, cols] = pair_attention(q[:, cols], k, v, allowed)


def out_kernel(
    moment, place_ref, mask_ref, q_ref, num_ref, den_ref, left_ref, right_ref, x_ref, near_ref, far_ref,
    o_ref, ctx_ref
):
    width = q_ref.shape[1]
    allowed = allowed_of(moment, True, place_ref, mask_ref)
    for lane in range(0, width, 2 * HD):
        cols = slice(lane, lane + 2 * HD)
        vcols = slice(width + lane, width + lane + 2 * HD)
        k = jnp.concatenate([left_ref[:, cols], right_ref[:, cols]], axis=0)
        v = jnp.concatenate([left_ref[:, vcols], right_ref[:, vcols]], axis=0)
        num, den = pair_attention(q_ref[:, cols], k, v, allowed)
        ctx_ref[:, cols] = ((num + num_ref[:, cols]) / (den + den_ref[:, cols])).astype(BF16)
    half = near_ref.shape[0]
    for cols, w_ref in ((slice(0, half), near_ref), (slice(half, 2 * half), far_ref)):
        update = matmul_nt(ctx_ref[...], w_ref[...])
        o_ref[:, cols] = (x_ref[:, cols].astype(F32) + update).astype(BF16)


def order_kernel(order_ref, frames_ref, *out_refs):
    seqs, rows, model = frames_ref.shape
    frames = frames_ref[...].reshape(seqs * rows, model)
    for lane in range(0, model, 256):
        source = lax.broadcasted_iota(jnp.int32, (model, 256), 0)
        hit = source == order_ref[:, lane : lane + 256]
        pick = jnp.where(hit, 1.0, 0.0).astype(BF16)
        moved = matmul(frames, pick).astype(BF16)
        for seq, out_ref in enumerate(out_refs):
            out_ref[:, lane : lane + 256] = moved[seq * rows : (seq + 1) * rows]


def reorder_kernel(order_ref, w_ref, out_ref):
    model = w_ref.shape[0]
    for row in range(0, model, 256):
        source = lax.broadcasted_iota(jnp.int32, (256, model), 1)
        hit = source == order_ref[row : row + 256, :]
        pick = jnp.where(hit, 1.0, 0.0).astype(BF16)
        out_ref[row : row + 256, :] = matmul(pick, w_ref[...]).astype(BF16)


def query_kernel(seg_ref, dec_ref, w_ref, q_ref):
    q_ref[...] = matmul(normed_rows(dec_ref[...]), w_ref[...]).astype(BF16)


def cross_kernel(place_ref, q_ref, w_ref, *refs):
    parts, out_ref = refs[:-1], refs[-1]
    owner = place_ref[0] == place_ref[1]
    rows = []
    for start in (0, 4):
        own, a, b, c = (ref[...] for ref in parts[start : start + 4])
        rows.append(jnp.where(owner, own, a + b + c))
    n = normed_rows(jnp.concatenate(rows, axis=0))
    width = q_ref.shape[1]
    both = matmul(n, w_ref[...]).astype(BF16)
    keys, values = both[:, :width], both[:, width:]
    tokens = q_ref.shape[0] // 4
    heads = 3
    lane = lax.broadcasted_iota(jnp.int32, (tokens, width), 1)
    near = lax.broadcasted_iota(jnp.int32, (tokens, 2 * HD), 1)
    sums = jnp.zeros((tokens, 2 * HD), F32)
    thirds = []
    for piece in range(4):
        q = q_ref[piece * tokens : (piece + 1) * tokens, :]
        spots = slice(piece * BLK, (piece + 1) * BLK)
        stacked = jnp.concatenate(
            [jnp.where(lane // HD == head, q, jnp.zeros_like(q)) for head in range(heads)], axis=0
        )
        weights = jnp.exp(matmul_nt(stacked, keys[spots]) * HD ** (-0.5))
        totals = jnp.sum(weights, axis=-1, keepdims=True)
        summed = matmul(weights.astype(BF16), values[spots])
        high = totals.astype(BF16).astype(F32)
        rest = totals - high
        for head in range(heads):
            mine = slice(head * tokens, (head + 1) * tokens)
            sums = jnp.where(near == 32 * piece + head, high[mine], sums)
            sums = jnp.where(near == 32 * piece + heads + head, rest[mine], sums)
        pair = jnp.where(near < HD, summed[:tokens, : 2 * HD], summed[tokens : 2 * tokens, : 2 * HD])
        out_ref[piece * tokens : (piece + 1) * tokens, :] = pair.astype(BF16)
        thirds.append(summed[2 * tokens :, 2 * HD :])
    at = 4 * tokens
    for block in range(2):
        shifted = pltpu.roll(thirds[2 + block], HD, 1)
        out_ref[at + block * tokens : at + (block + 1) * tokens, :] = jnp.where(
            near < HD, thirds[block], shifted
        ).astype(BF16)
    out_ref[at + 2 * tokens :, :] = sums.astype(BF16)


def combine_kernel(
    place_ref, span_ref, parts_ref, cot_ref, ctx_ref, grad_ref, pair_ref, third_ref, sum_ref, all_ref
):
    shards = parts_ref.shape[0]
    tokens = pair_ref.shape[1]
    heads = 3
    for ref in (pair_ref, third_ref, sum_ref):
        ref[...] = jnp.zeros_like(ref)
    lane = lax.broadcasted_iota(jnp.int32, (tokens, 2 * HD), 1)
    for shard in range(shards):
        sums = parts_ref[shard, 6 * tokens : 7 * tokens, :].astype(F32)
        for seq in range(MB):
            for block in range(2):
                segment = span_ref[seq * 2 * shards + shard * 2 + block]
                spot = segment * MB + seq
                piece = seq * 2 + block
                pair = parts_ref[shard, piece * tokens : (piece + 1) * tokens, :]
                third = parts_ref[shard, (4 + block) * tokens : (5 + block) * tokens, :]
                pair_ref[spot] = pair_ref[spot] + pair.astype(F32)
                third_ref[spot] = third_ref[spot] + third.astype(F32)
                sum_ref[spot] = sum_ref[spot] + jnp.where(lane // 32 == piece, sums, 0.0)
    count = shards * tokens
    near = lax.broadcasted_iota(jnp.int32, (count, 2 * HD), 1)
    for seq in range(MB):

        def taken(ref):
            return ref[...].reshape(shards, MB, tokens, 2 * HD)[:, seq].reshape(count, 2 * HD)

        sums = taken(sum_ref)

        def total(head):
            at = 64 * seq + head
            spots = (at, at + heads, at + 32, at + 32 + heads)
            return sum(sums[:, spot : spot + 1] for spot in spots)

        pair = taken(pair_ref) / jnp.where(near < HD, total(0), total(1))
        third = taken(third_ref) / total(2)
        if seq:
            third = pltpu.roll(third, HD, 1)
        third = jnp.where(near < HD, third, 0.0)
        rows = slice(seq * tokens, (seq + 1) * tokens)
        all_ref[:, rows, : 2 * HD] = pair.astype(BF16).reshape(shards, tokens, 2 * HD)
        all_ref[:, rows, 2 * HD :] = third.astype(BF16).reshape(shards, tokens, 2 * HD)
    ctx_ref[...] = all_ref[place_ref[2]][:, : heads * HD]
    context = all_ref[...].reshape(shards * MB * tokens, 4 * HD)
    grad = lax.dot_general(
        cot_ref[...], context, (((0,), (0,)), ((), ())), preferred_element_type=F32
    )
    grad_ref[...] = grad.reshape(grad_ref.shape).astype(BF16)


def columns_kernel(place_ref, cot_ref, out_ref):
    cols = cot_ref.shape[1]
    lanes = out_ref.shape[1]
    each = place_ref[3]
    row = lax.broadcasted_iota(jnp.int32, (cols, lanes), 0)
    lane = lax.broadcasted_iota(jnp.int32, (cols, lanes), 1)
    inside = lane % 16
    hit = (row == (lane // 16) * place_ref[4] + place_ref[2] * each + inside) & (inside < each)
    out_ref[...] = matmul(cot_ref[...], jnp.where(hit, 1.0, 0.0).astype(BF16)).astype(BF16)


def shape(dims, dtype=BF16):
    return jax.ShapeDtypeStruct(dims, dtype)


def per_device(
    frames,
    block_mask,
    span_segment,
    dec_states,
    enc_qkv,
    enc_out,
    cross_query,
    cross_key,
    cross_value,
    cotangent,
):
    sections = lax.axis_size("section")
    shards = lax.axis_size("tm")
    groups = lax.axis_size("dp")
    section = lax.axis_index("section")
    shard = lax.axis_index("tm")
    model = frames.shape[2]
    width = enc_out.shape[1]
    head_width = cross_query.shape[1]
    padded = 256

    def pad_lanes(w):
        return jnp.pad(w, ((0, 0), (0, padded - w.shape[1])))

    def around(value, axis, size, step):
        return lax.ppermute(value, axis, [(i, (i + step) % size) for i in range(size)])

    own = jnp.concatenate([enc_qkv[0], enc_out[0].T], axis=1)
    lanes = own.reshape(-1, 128)
    block = lax.all_to_all(
        jnp.broadcast_to(lanes[None], (groups,) + lanes.shape), "dp", 0, 0, tiled=True
    ).reshape(groups * own.shape[0], own.shape[1])
    chips = shards // 2
    ring, source = [block], [shard]
    ends = []
    for step in (2, -2):
        moving = block
        for hop in range(chips // 2 - 1):
            moving = around(moving, "tm", shards, step)
            ring.append(moving)
            source.append((shard - step * (hop + 1)) % shards)
        ends.append(moving)
    cut = block.shape[0] * 3 // 5
    ring.append(around(ends[0][:cut], "tm", shards, 2))
    ring.append(around(ends[1][cut:], "tm", shards, -2))
    source.append((shard + chips) % shards)
    source = jnp.stack(source + [place ^ 1 for place in source])
    each = model // (groups * shards)
    slots = jnp.arange(groups)
    order = (slots[None, :, None] * shards + source[:, None, None]) * each + jnp.arange(each)
    order = order.reshape(-1).astype(jnp.int32)

    inputs = pl.pallas_call(
        order_kernel,
        out_shape=(shape(frames.shape[1:]),) * MB,
        in_specs=[VMEM, VMEM],
        out_specs=(VMEM,) * MB,
        compiler_params=PARAMS,
        name="order",
    )(order.reshape(1, -1), frames)

    ring[-1], *inputs = lax.optimization_barrier((ring[-1], *inputs))
    half = model // 2
    q_near, kv_near, out_near = pl.pallas_call(
        join_kernel,
        out_shape=(shape((half, width)), shape((half, 2 * width)), shape((half, width))),
        in_specs=[pl.BlockSpec(memory_space=pl.ANY)] * len(ring),
        out_specs=(VMEM,) * 3,
        scratch_shapes=[pltpu.SemaphoreType.DMA((3, len(ring)))],
        compiler_params=pltpu.CompilerParams(),
        name="join",
    )(*ring)
    swap = [(i, i ^ 1) for i in range(shards)]
    kv_far, q_far, out_far = (lax.ppermute(w, "tm", swap) for w in (kv_near, q_near, out_near))

    cross = jnp.concatenate([pad_lanes(w) for w in (cross_key, cross_value, cross_query)], axis=1)
    cross = lax.all_gather(cross, ("dp", "tm"), axis=0, tiled=True)
    tokens_all = lax.all_gather(
        jnp.concatenate([dec_states, cotangent], axis=1), "tm", axis=0, tiled=True
    )

    place = jnp.stack(
        [
            section,
            jnp.int32(sections - 1),
            shard,
            jnp.int32(each),
            jnp.int32(each * shards),
            jnp.int32(shards - 1),
        ]
    ).astype(jnp.int32)
    mask = block_mask.reshape(-1)
    up = [(i, i + 1) for i in range(shards - 1)]
    down = [(i + 1, i) for i in range(shards - 1)]
    onward = [(i, i + 1) for i in range(sections - 1)]
    rows = frames.shape[1]
    tokens = dec_states.shape[0] // MB
    carried = inputs[0]
    memory = []
    for moment in range(MB + sections - 1):
        if moment == 1:
            carried, cross = lax.optimization_barrier((carried, cross))
        if 0 < moment < MB:
            carried = jnp.where(section == 0, inputs[moment], carried)
        if moment == 2:
            w_cross = pl.pallas_call(
                reorder_kernel,
                grid=(1,),
                out_shape=shape((model, 2 * padded)),
                in_specs=[
                    pl.BlockSpec((model, 1), lambda i: (0, 0)),
                    pl.BlockSpec((model, 2 * padded), lambda i: (0, 0)),
                ],
                out_specs=pl.BlockSpec((model, 2 * padded), lambda i: (0, 0)),
                compiler_params=PARAMS,
                name="reorder",
            )(order.reshape(-1, 1), cross)
            carried, w_cross = lax.optimization_barrier((carried, w_cross))
        if moment == 3:
            mine = lax.dynamic_slice_in_dim(span_segment, shard * 2, 2, axis=1).reshape(-1)
            queries = pl.pallas_call(
                query_kernel,
                grid_spec=pltpu.PrefetchScalarGridSpec(
                    num_scalar_prefetch=1,
                    grid=(4,),
                    in_specs=[
                        pl.BlockSpec((tokens, model), lambda i, seg: (seg[i] * MB + i // 2, 0)),
                        pl.BlockSpec((model, padded), lambda i, seg: (0, 2)),
                    ],
                    out_specs=pl.BlockSpec((tokens, padded), lambda i, seg: (i, 0)),
                ),
                out_shape=shape((4 * tokens, padded)),
                compiler_params=PARAMS,
                name="queries",
            )(mine, tokens_all, cross)
            carried, queries = lax.optimization_barrier((carried, queries))
        if moment == 4:
            cot_cols = pl.pallas_call(
                columns_kernel,
                grid=(1,),
                out_shape=shape((shards * MB * tokens, groups * 16)),
                in_specs=[
                    SMEM,
                    pl.BlockSpec((shards * MB * tokens, model), lambda i: (0, 1)),
                ],
                out_specs=pl.BlockSpec((shards * MB * tokens, groups * 16), lambda i: (0, 0)),
                compiler_params=PARAMS,
                name="columns",
            )(place, tokens_all)
            carried, cot_cols = lax.optimization_barrier((carried, cot_cols))

        n, first, last = pl.pallas_call(
            kv_kernel,
            out_shape=(shape((rows, model)), shape((BLK, 2 * width)), shape((BLK, 2 * width))),
            in_specs=[VMEM] * 3,
            out_specs=(VMEM, VMEM, VMEM),
            compiler_params=PARAMS,
            name="keys_values",
        )(carried, kv_near, kv_far)
        left = lax.ppermute(last, "tm", up)
        right = lax.ppermute(first, "tm", down)
        q, num, den = pl.pallas_call(
            functools.partial(own_kernel, moment),
            out_shape=(shape((rows, width)), shape((rows, width), F32), shape((rows, width), F32)),
            in_specs=[SMEM, SMEM] + [VMEM] * 5,
            out_specs=(VMEM, VMEM, VMEM),
            compiler_params=PARAMS,
            name="own_blocks",
        )(place, mask, n, first, last, q_near, q_far)
        if moment == sections:
            q, relayed = lax.optimization_barrier((q, relayed))
            memory.append(lax.ppermute(relayed, "section", [(0, 1)]))
        finished = pl.pallas_call(
            functools.partial(out_kernel, moment),
            out_shape=shape((rows, model)),
            in_specs=[SMEM, SMEM] + [VMEM] * 8,
            out_specs=VMEM,
            scratch_shapes=[pltpu.VMEM((rows, width), BF16)],
            compiler_params=PARAMS,
            name="layer_out",
        )(place, mask, q, num, den, left, right, carried, out_near, out_far)
        if moment >= sections - 1:
            targets = (0, 2) if moment == sections - 1 else (1, 2, 0)
            sent = [lax.ppermute(finished, "section", [(sections - 1, t)]) for t in targets]
            if moment == sections - 1:
                relayed = sent[0]
            memory += [finished] + sent
        if moment < MB + sections - 2:
            carried = lax.ppermute(finished, "section", onward)

    pieces = pl.pallas_call(
        cross_kernel,
        out_shape=shape((7 * tokens, 2 * HD)),
        in_specs=[SMEM] + [VMEM] * 10,
        out_specs=VMEM,
        compiler_params=PARAMS,
        name="cross",
    )(place, queries, w_cross, *memory)
    everyone = lax.all_gather(pieces, "tm", axis=0)
    context, grad = pl.pallas_call(
        combine_kernel,
        out_shape=(
            shape((MB * tokens, head_width)),
            shape((groups, 16, padded)),
        ),
        in_specs=[SMEM, SMEM, VMEM, VMEM],
        out_specs=(VMEM, VMEM),
        scratch_shapes=[pltpu.VMEM((shards * MB, tokens, 2 * HD), F32)] * 3
        + [pltpu.VMEM((shards, MB * tokens, padded), BF16)],
        compiler_params=PARAMS,
        name="combine",
    )(place, span_segment.reshape(-1), everyone, cot_cols)
    grad = lax.all_to_all(grad, "dp", 0, 0, tiled=True)
    grad_shard = jnp.sum(grad.astype(F32), axis=0)[:each, :head_width].T
    return (context, grad_shard)


def solution(mesh):
    in_specs = (
        P("dp", "tm", None),
        P("dp", "tm", None),
        P("dp", None),
        P(("dp", "tm"), None),
        P("section", ("dp", "tm"), None),
        P("section", None, ("dp", "tm")),
        P(("dp", "tm"), "section"),
        P(("dp", "tm"), "section"),
        P(("dp", "tm"), "section"),
        P(("dp", "tm"), None),
    )
    out_specs = (P(("dp", "tm"), "section"), P("section", ("dp", "tm")))
    return jax.shard_map(
        per_device, mesh=mesh, in_specs=in_specs, out_specs=out_specs, check_vma=False
    )
```
